256 devices in a mesh: feat: 64 (over z, y, core), layer: 4 (over x).
Axes of the slice: x: 4, y: 4, z: 8, core: 2. Of those that a mesh axis runs over, the one named last changes fastest.
Arguments:
- resid_in: bfloat16 [4, 512, 2304], P('layer', 'feat'), may hold values from -6 to 6
- enc_weight: bfloat16 [4, 2304, 32768], P('layer', None, 'feat'), may hold values from -0.125 to 0.125
- enc_bias: float32 [4, 32768], P('layer', 'feat'), may hold values from -3 to 3
- dec_weight: bfloat16 [4, 4, 32768, 2304], P('layer', None, 'feat'), may hold values from -0.03125 to 0.03125
- dec_bias: float32 [4, 2304], P('layer'), may hold values from -3 to 3
Outputs:
- recon: bfloat16 [4, 512, 2304], P('layer', 'feat')
The draws below stay inside these ranges and needn't reach their ends.
All inputs are finite; a program needn't handle non-finite values.
Results may differ from the reference program's by a relative error of at most 0.0046.
Values may be sent and summed in bfloat16 or wider, within the bound.
A program may use at most 128 MiB of HBM per device.

```python
import jax
import jax.numpy as jnp

D = 2304
TOKENS = 512
F = 32768
LAYERS = 4


def level_of(stream_key, shape, pieces, smallest, top_value):
    factor_of = 1.0
    for axis_at, parts in pieces:
        heights = jax.random.uniform(jax.random.fold_in(jax.random.fold_in(stream_key, 6), axis_at), (parts,), jnp.float32, smallest / len(pieces), top_value / len(pieces))
        factor_of = factor_of * jnp.repeat(jnp.exp(heights), shape[axis_at] // parts).reshape((-1,) + (1,) * (len(shape) - 1 - axis_at))
    return factor_of


def bell_draw(rng, dims, scale, reach, split=(), held_as=jnp.bfloat16):
    entries = scale * jax.random.normal(rng, dims, jnp.float32)
    if split:
        entries = entries * level_of(rng, dims, split, -0.22, 0.18)
    return jnp.clip(entries, -reach, reach).astype(held_as)


def setup_inputs(seed: int = 0) -> dict:
    splits = jax.random.split(jax.random.key(seed), 6)
    return {
        "resid_in": bell_draw(splits[0], (LAYERS, TOKENS, D), 1.0, 6.0, ((0, 4), (1, 64))),
        "enc_weight": bell_draw(splits[1], (LAYERS, D, F), D ** -0.5, 0.125, ((0, 4), (2, 64))),
        "enc_bias": bell_draw(splits[2], (LAYERS, F), 0.5, 3.0, ((0, 4), (1, 64)), jnp.float32),
        "dec_weight": bell_draw(splits[3], (LAYERS, LAYERS, F, D), F ** -0.5, 0.03125, ((0, 4), (2, 64))),
        "dec_bias": bell_draw(splits[4], (LAYERS, D), 0.5, 3.0, ((0, 4),), jnp.float32),
    }


def reference(resid_in, enc_weight, enc_bias, dec_weight, dec_bias):
    actives = []
    for layer_idx in range(LAYERS):
        preact = jnp.dot(resid_in[layer_idx], enc_weight[layer_idx], preferred_element_type=jnp.float32) + enc_bias[layer_idx][None, :]
        actives.append(jnp.maximum(preact, 0.0).astype(jnp.bfloat16))
    outputs = []
    for target in range(LAYERS):
        summed = jnp.zeros((TOKENS, D), jnp.float32)
        for source in range(target + 1):
            summed = summed + jnp.dot(actives[source], dec_weight[source, target], preferred_element_type=jnp.float32)
        outputs.append((summed + dec_bias[target][None, :]).astype(jnp.bfloat16))
    return jnp.stack(outputs, axis=0)
```

```python
import jax
import jax.numpy as jnp
from jax import lax
from jax.experimental import pallas as pl
from jax.experimental.pallas import tpu as pltpu
from jax.sharding import Mesh
from jax.sharding import PartitionSpec as P

FEAT = ("z", "y", "c")
MESH = pl.DeviceIdType.MESH
Z, Y, C, X = 8, 4, 2, 4
SIZE = {"z": Z, "y": Y, "c": C, "x": X}
ROWS = 8
D = 2304
FEATS = 512
TILE = 256
GATHER_SPLIT = 1152
B_COLS = 1280
A_COLS = D - B_COLS


class Group:
    def __init__(self, first, start, width, ks):
        self.first, self.second = first, "y" if first == "z" else "z"
        self.start, self.width, self.ks = start, width, ks
        self.n1, self.n2 = SIZE[self.first], SIZE[self.second]

    def scratch(self):
        k, n1, n2, w = self.ks, self.n1, self.n2, self.width
        return [
            pltpu.VMEM((k, n1 - 1, n2, ROWS, w), jnp.bfloat16),
            pltpu.VMEM((k, n1 - 1, n2, ROWS, w), jnp.bfloat16),
            pltpu.VMEM((k, n2, ROWS, w), jnp.float32),
            pltpu.VMEM((k, n2 - 1, ROWS, w), jnp.bfloat16),
            pltpu.VMEM((k, n2 - 1, ROWS, w), jnp.bfloat16),
            pltpu.SemaphoreType.DMA((k, n1 - 1)),
            pltpu.SemaphoreType.DMA((k, n1 - 1)),
            pltpu.SemaphoreType.DMA((k, n2 - 1)),
            pltpu.SemaphoreType.DMA((k, n2 - 1)),
        ]

    def bind(self, refs):
        (self.s1, self.r1, self.t, self.s2, self.r2, self.ss1, self.rs1, self.ss2, self.rs2) = refs


def groups():
    return [
        Group("y", 0, 768, 4),
        Group("z", 768, 512, 4),
        Group("y", B_COLS, 512, 2),
        Group("z", B_COLS + 512, 512, 2),
    ]


def shifted(axis, step):
    return lax.rem(lax.axis_index(axis) + step + 2 * SIZE[axis], SIZE[axis])


def remote(src, dst, send, recv, axis, step):
    return pltpu.make_async_remote_copy(
        src_ref=src, dst_ref=dst, send_sem=send, recv_sem=recv,
        device_id={axis: shifted(axis, step)}, device_id_type=MESH,
    )


def kernel(x_ref, enc_ref, eb_ref, dec_ref, db_ref, o_ref, wenc, wdec, ebv, xg, act, part, mvs, mvr, fin, fsend, frecv,
           local_sem, w_ss, w_rs, ay_ss, ay_rs, az_ss, az_rs, bz_ss, bz_rs, by_ss, by_rs, mv_ss, mv_rs, f_ss, f_rs, *rest):
    gs = groups()
    for i, g in enumerate(gs):
        g.bind(rest[9 * i : 9 * i + 9])
    z, y, c, l = (lax.axis_index(a) for a in ("z", "y", "c", "x"))
    n_b = X - l
    n_a = jnp.where(l < 2, 2, 1)

    locals_ = [
        pltpu.make_async_copy(enc_ref.at[0], wenc.at[c], local_sem.at[0]),
        pltpu.make_async_copy(eb_ref, ebv.at[c], local_sem.at[1]),
        pltpu.make_async_copy(x_ref.at[0], xg.at[y, z], local_sem.at[2]),
    ]
    for cp in locals_:
        cp.start()

    def dec_local(k):
        return pltpu.make_async_copy(dec_ref.at[0, l + k], wdec.at[k, c], local_sem.at[3 + k])

    def dec_push(k):
        return remote(dec_ref.at[0, l + k], wdec.at[k, c], w_ss.at[2 + k], w_rs.at[2 + k], "c", 1)

    def each_k(fn, order=(1, 3, 0, 2)):
        for k in order:
            if k == 0:
                fn(0)
            else:
                pl.when(l + k < X)(lambda k=k: fn(k))

    each_k(lambda k: dec_local(k).start())

    bar = pltpu.get_barrier_semaphore()
    peers = [("c", 1)] + [("y", i) for i in (1, 2, 3)] + [("z", i) for i in range(1, 8)] + [("x", i) for i in (1, 2, 3)]
    for a, i in peers:
        pl.semaphore_signal(bar, inc=1, device_id={a: shifted(a, i)}, device_id_type=MESH)
    pl.semaphore_wait(bar, len(peers))

    lo, hi = pl.ds(0, GATHER_SPLIT), pl.ds(GATHER_SPLIT, D - GATHER_SPLIT)

    def gy(i):
        return remote(x_ref.at[0, :, lo], xg.at[y, z, :, lo], ay_ss.at[i - 1], ay_rs.at[i - 1], "y", i)

    def gz(i):
        return remote(x_ref.at[0, :, hi], xg.at[y, z, :, hi], bz_ss.at[i - 1], bz_rs.at[i - 1], "z", i)

    def chain(s, j, long):
        step = (1 if long else -1) * (1 if j % 2 == 0 else -1)
        zb = shifted("z", -step * s)
        yb = shifted("y", -j)
        slot = (s if long else 4 + s) * 4 + j
        src = x_ref.at[0, :, lo] if s == 0 and j == 0 else xg.at[yb, zb, :, lo]
        return remote(src, xg.at[yb, zb, :, lo], az_ss.at[slot], az_rs.at[slot], "z", step)

    def hop(s, j):
        for long, hops in ((True, 4), (False, 3)):
            if s > 0 and s <= hops:
                chain(s - 1, j, long).wait_recv()
            if s < hops:
                chain(s, j, long).start()

    def across(j, i):
        zb = shifted("z", -j)
        src = x_ref.at[0, :, hi] if j == 0 else xg.at[y, zb, :, hi]
        return remote(src, xg.at[y, zb, :, hi], by_ss.at[j * 3 + i - 1], by_rs.at[j * 3 + i - 1], "y", i)

    def spread(j):
        for i in (1, 3, 2):
            across(j, i).start()

    for i in (1, 3, 2):
        gy(i).start()
    for i in (4, 3, 5, 2, 6, 1, 7):
        gz(i).start()
    hop(0, 0)
    spread(0)

    enc_push = remote(enc_ref.at[0], wenc.at[c], w_ss.at[0], w_rs.at[0], "c", 1)
    eb_push = remote(eb_ref, ebv.at[c], w_ss.at[1], w_rs.at[1], "c", 1)
    enc_push.start()
    eb_push.start()
    each_k(lambda k: dec_push(k).start())

    def take_y(i):
        gy(i).wait_recv()
        hop(0, i)

    def take_z(j):
        gz(j).wait_recv()
        spread(j)

    take_y(1), take_y(3), take_z(1), take_z(7), hop(1, 0), take_y(2), take_z(2), take_z(6), hop(1, 1), hop(1, 3)
    take_z(3), take_z(5), hop(1, 2), take_z(4)
    for s in (2, 3, 4):
        for j in (0, 1, 3, 2):
            hop(s, j)
    for j in (0, 1, 7, 2, 6, 3, 5, 4):
        for i in (1, 3, 2):
            across(j, i).wait_recv()
    for cp in locals_:
        cp.wait()
    enc_push.wait_recv()
    eb_push.wait_recv()

    rows = xg[...].astype(jnp.float32).reshape(Z * Y * ROWS, D).astype(jnp.bfloat16)
    for side in range(C):
        for n in range(FEATS // TILE):
            at = pl.ds(n * TILE, TILE)
            pre = jnp.dot(rows, wenc[side, :, at], preferred_element_type=jnp.float32) + ebv[side, :, at]
            act[:, pl.ds(side * FEATS + n * TILE, TILE)] = jnp.maximum(pre, 0.0).astype(jnp.bfloat16)

    def product(k, col):
        at = pl.ds(col, TILE)
        weight = wdec[k, :, :, at].reshape(C * FEATS, TILE)
        out = jnp.dot(act[...], weight, preferred_element_type=jnp.float32)
        return out.reshape(Y, Z, ROWS, TILE)

    def dec_ready(k):
        dec_local(k).wait()
        dec_push(k).wait_recv()

    def move(i, n):
        at = pl.ds(n * TILE, TILE)
        return remote(mvs.at[i, :, :, :, at], mvr.at[i, :, :, :, at], mv_ss.at[i, n], mv_rs.at[i, n], "x", 1 - 2 * i)

    def moved(k):
        dec_ready(k)
        i = k // 2
        for n in range(A_COLS // TILE):
            mvs[i, :, :, :, pl.ds(n * TILE, TILE)] = product(k, B_COLS + n * TILE).astype(jnp.bfloat16)
            move(i, n).start()

    each_k(moved, (1, 3))

    def own1(g, k, d):
        cols = pl.ds(g.start, g.width)
        return part[k, d, :, :, cols] if g.first == "y" else part[k, :, d, :, cols]

    def own2(g, j, d):
        return g.t[j, d]

    def send_copy(g, stage, j, slot, step):
        s, r, ss, rs = (g.s1, g.r1, g.ss1, g.rs1) if stage == 1 else (g.s2, g.r2, g.ss2, g.rs2)
        return remote(s.at[j, slot], r.at[j, slot], ss.at[j, slot], rs.at[j, slot], g.first if stage == 1 else g.second, step)

    def ring(g, stage, j, k, s):
        axis, size = (g.first, g.n1) if stage == 1 else (g.second, g.n2)
        own = (lambda d: own1(g, k, d)) if stage == 1 else (lambda d: own2(g, j, d))
        sref, rref = (g.s1, g.r1) if stage == 1 else (g.s2, g.r2)
        sign = 1 - 2 * lax.rem(j, 2)
        half = size // 2
        for hops, step, base in ((half, sign, 0), (half - 1, -sign, half)):
            if s > 0 and s <= hops:
                send_copy(g, stage, j, base + s - 1, step).wait_recv()
            if s < hops:
                msg = own(shifted(axis, step * (hops - s)))
                if s > 0:
                    msg = msg + rref[j, base + s - 1].astype(jnp.float32)
                sref[j, base + s] = msg.astype(jnp.bfloat16)
                send_copy(g, stage, j, base + s, step).start()
        if s == half:
            me = lax.axis_index(axis)
            total = own(me) + rref[j, half - 1].astype(jnp.float32) + rref[j, size - 2].astype(jnp.float32)
            if stage == 1:
                g.t[j] = total
            else:
                fin[k, :, pl.ds(g.start, g.width)] = total

    def direct_send(g, j):
        for o in range(1, g.n2):
            g.s2[j, o - 1] = own2(g, j, shifted(g.second, o)).astype(jnp.bfloat16)
            send_copy(g, 2, j, o - 1, o).start()

    def direct_sum(g, j, k):
        total = own2(g, j, lax.axis_index(g.second))
        for o in range(1, g.n2):
            send_copy(g, 2, j, o - 1, o).wait_recv()
            total = total + g.r2[j, o - 1].astype(jnp.float32)
        fin[k, :, pl.ds(g.start, g.width)] = total

    by, bz, ay, az = gs

    def loop_b(fn):
        def body(k, carry):
            fn(k)
            return carry

        lax.fori_loop(0, n_b, body, 0)

    def loop_a(fn):
        def body(j, carry):
            fn(j, 2 * j)
            return carry

        lax.fori_loop(0, n_a, body, 0)

    def compute_b(k):
        for n in range(B_COLS // TILE):
            part[k, :, :, :, pl.ds(n * TILE, TILE)] = product(k, n * TILE)
        ring(by, 1, k, k, 0)
        ring(bz, 1, k, k, 0)

    def first_b(k):
        @pl.when(lax.rem(k, 2) == 0)
        def _():
            dec_ready(k)

        compute_b(k)

    loop_b(first_b)

    def compute_a(j, k):
        for n in range(A_COLS // TILE):
            at = B_COLS + n * TILE
            part[k, :, :, :, pl.ds(at, TILE)] = product(k, at)

    loop_a(compute_a)

    @pl.when(l < 2)
    def _():
        ring(ay, 1, 1, 2, 0)
        ring(az, 1, 1, 2, 0)

    def step_b(s):
        def fn(k):
            if s <= 2:
                ring(by, 1, k, k, s)
            ring(bz, 1, k, k, s)
            if s == 2:
                ring(by, 2, k, k, 0)
            if s == 4:
                ring(bz, 2, k, k, 0)

        loop_b(fn)

    step_b(1)
    step_b(2)

    def join(i):
        for n in range(A_COLS // TILE):
            move(i, n).wait_recv()
            at = pl.ds(B_COLS + n * TILE, TILE)
            part[0, :, :, :, at] = part[0, :, :, :, at] + mvr[i, :, :, :, pl.ds(n * TILE, TILE)].astype(jnp.float32)

    pl.when(l > 0)(lambda: join(0))
    pl.when(l == X - 1)(lambda: join(1))
    ring(ay, 1, 0, 0, 0)
    ring(az, 1, 0, 0, 0)

    step_b(3)
    step_b(4)

    def step_a(s):
        def fn(j, k):
            if s <= 2:
                ring(ay, 1, j, k, s)
            ring(az, 1, j, k, s)
            if s == 2:
                direct_send(ay, j)
            if s == 4:
                direct_send(az, j)

        loop_a(fn)

    def tail_b(s):
        def fn(k):
            ring(by, 2, k, k, s)
            if s <= 2:
                ring(bz, 2, k, k, s)

        loop_b(fn)

    for s in (1, 2, 3, 4):
        step_a(s)
        tail_b(s)

    def late(k, is_a):
        at = pl.ds(B_COLS, A_COLS) if is_a else pl.ds(0, B_COLS)
        slot = 3 if is_a else k - 1
        return remote(fsend.at[k - 1, :, at], frecv.at[k - 1, :, at], f_ss.at[slot], f_rs.at[slot], "x", k)

    def send_late(k, is_a):
        at = pl.ds(B_COLS, A_COLS) if is_a else pl.ds(0, B_COLS)
        fsend[k - 1, :, at] = fin[k, :, at].astype(jnp.bfloat16)
        late(k, is_a).start()

    each_k(lambda k: send_late(k, False), (1, 2, 3))

    def end_a(j, k):
        direct_sum(ay, j, k)
        direct_sum(az, j, k)

    loop_a(end_a)
    pl.when(l < 2)(lambda: send_late(2, True))

    def take_late(k, is_a):
        late(k, is_a).wait_recv()
        at = pl.ds(B_COLS, A_COLS) if is_a else pl.ds(0, B_COLS)
        fin[0, :, at] = fin[0, :, at] + frecv[k - 1, :, at].astype(jnp.float32)

    for k in (1, 2, 3):
        pl.when(l >= k)(lambda k=k: take_late(k, False))
    pl.when(l >= 2)(lambda: take_late(2, True))
    o_ref[0] = (fin[0] + db_ref[...]).astype(jnp.bfloat16)

    for i in (1, 2, 3):
        gy(i).wait_send()
        for j in range(Z):
            across(j, i).wait_send()
    for i in range(1, Z):
        gz(i).wait_send()
    for j in range(Y):
        for s in range(4):
            chain(s, j, True).wait_send()
            if s < 3:
                chain(s, j, False).wait_send()
    enc_push.wait_send()
    eb_push.wait_send()
    each_k(lambda k: dec_push(k).wait_send())

    def moves_left(k):
        for n in range(A_COLS // TILE):
            move(k // 2, n).wait_send()

    each_k(moves_left, (1, 3))
    each_k(lambda k: late(k, False).wait_send(), (1, 2, 3))
    pl.when(l < 2)(lambda: late(2, True).wait_send())

    def drain(g, j):
        for slot in range(g.n1 - 1):
            send_copy(g, 1, j, slot, 1).wait_send()
        for slot in range(g.n2 - 1):
            send_copy(g, 2, j, slot, 1).wait_send()

    loop_b(lambda k: (drain(by, k), drain(bz, k)))
    loop_a(lambda j, k: (drain(ay, j), drain(az, j)))


def per_device(resid_in, enc_weight, enc_bias, dec_weight, dec_bias):
    dma = pltpu.SemaphoreType.DMA
    scratch = [
        pltpu.VMEM((C, D, FEATS), jnp.bfloat16),
        pltpu.VMEM((X, C, FEATS, D), jnp.bfloat16),
        pltpu.VMEM((C, 1, FEATS), jnp.float32),
        pltpu.VMEM((Y, Z, ROWS, D), jnp.bfloat16),
        pltpu.VMEM((Z * Y * ROWS, C * FEATS), jnp.bfloat16),
        pltpu.VMEM((X, Y, Z, ROWS, D), jnp.float32),
        pltpu.VMEM((2, Y, Z, ROWS, A_COLS), jnp.bfloat16),
        pltpu.VMEM((2, Y, Z, ROWS, A_COLS), jnp.bfloat16),
        pltpu.VMEM((X, ROWS, D), jnp.float32),
        pltpu.VMEM((X - 1, ROWS, D), jnp.bfloat16),
        pltpu.VMEM((X - 1, ROWS, D), jnp.bfloat16),
        dma((7,)),
        dma((6,)), dma((6,)),
        dma((3,)), dma((3,)),
        dma((28,)), dma((28,)),
        dma((7,)), dma((7,)),
        dma((24,)), dma((24,)),
        dma((2, A_COLS // TILE)), dma((2, A_COLS // TILE)),
        dma((4,)), dma((4,)),
    ]
    for g in groups():
        scratch += g.scratch()
    anywhere = pl.BlockSpec(memory_space=pl.ANY)
    return pl.pallas_call(
        kernel,
        out_shape=jax.ShapeDtypeStruct((1, ROWS, D), jnp.bfloat16),
        in_specs=[anywhere, anywhere, anywhere, anywhere, pl.BlockSpec(memory_space=pltpu.VMEM)],
        out_specs=pl.BlockSpec(memory_space=pltpu.VMEM),
        scratch_shapes=scratch,
        compiler_params=pltpu.CompilerParams(collective_id=0, has_side_effects=True, vmem_limit_bytes=67043328),
        name="transcoder",
    )(resid_in, enc_weight, enc_bias, dec_weight, dec_bias)


def solution(mesh):
    finer = Mesh(mesh.devices.reshape(Z, Y, C, X), ("z", "y", "c", "x"))
    return jax.shard_map(
        per_device,
        mesh=finer,
        in_specs=(
            P("x", FEAT, None),
            P("x", None, FEAT),
            P("x", FEAT),
            P("x", None, FEAT, None),
            P("x", None),
        ),
        out_specs=P("x", FEAT, None),
        check_vma=False,
    )
```

```python
import jax
import jax.numpy as jnp
from jax import lax
from jax.experimental import pallas as pl
from jax.experimental.pallas import tpu as pltpu
from jax.sharding import Mesh
from jax.sharding import PartitionSpec as P

FEAT = ("z", "y", "c")
MESH = pl.DeviceIdType.MESH
Z, Y, C, X = 8, 4, 2, 4
SIZE = {"z": Z, "y": Y, "c": C, "x": X}
ROWS = 8
D = 2304
FEATS = 512
TILE = 256
GATHER_SPLIT = 896
B_COLS = 1280
A_COLS = D - B_COLS

ORDER = (
    (1,1), (1,3), (0,1), (0,2), (2,2), (0,3), (0,0), (4,1,1,1,1,1), (4,1,1,1,0,1), (4,0,1,1,1,1), (4,0,1,1,0,1), (2,0), (4,1,1,2,1,1),
    (4,1,1,2,0,1), (4,0,1,2,1,1), (4,0,1,2,0,1), (4,1,1,3,1,1), (4,1,1,3,0,1), (4,1,1,0,1,1), (4,1,1,0,0,1), (4,2,1,2,1,1),
    (4,2,1,2,0,1), (4,1,1,1,1,2), (4,1,1,1,0,2), (4,1,1,2,1,2), (4,1,1,2,0,2), (4,0,1,3,1,1), (4,0,1,3,0,1), (4,1,1,3,1,2),
    (4,1,1,3,0,2), (3,2), (4,0,1,0,1,1), (4,0,1,0,0,1), (4,1,1,0,1,2), (4,1,1,0,0,2), (4,0,1,1,1,2), (4,0,1,2,1,2), (4,1,1,1,1,3),
    (4,1,1,1,0,3), (4,1,1,2,1,3), (4,1,1,2,0,3), (4,1,1,3,1,3), (4,1,1,3,0,3), (4,2,1,2,1,2), (4,1,1,0,1,3), (4,1,1,0,0,3),
    (4,2,1,0,1,1), (4,0,1,3,1,2), (4,0,1,0,1,2), (5,0,1), (4,2,1,0,0,1), (4,1,1,1,1,4), (4,1,1,2,1,4), (5,0,2), (4,1,1,3,1,4),
    (4,2,1,0,1,2), (4,1,1,0,1,4), (5,1,1), (5,1,2), (5,1,3), (5,2,2), (5,1,0), (5,0,3), (5,0,0), (5,2,0),
)

class Group:
    def __init__(self, first, start, width, ks, direct):
        self.first, self.second = first, "y" if first == "z" else "z"
        self.start, self.width, self.ks = start, width, ks
        self.n1, self.n2 = SIZE[self.first], SIZE[self.second]
        self.direct = direct

    def scratch(self):
        k, n1, n2, w = self.ks, self.n1, self.n2, self.width
        return [
            pltpu.VMEM((k, n1 - 1, n2, ROWS, w), jnp.bfloat16),
            pltpu.VMEM((k, n1 - 1, n2, ROWS, w), jnp.bfloat16),
            pltpu.VMEM((k, n2, ROWS, w), jnp.float32),
            pltpu.VMEM((k, n2 - 1, ROWS, w), jnp.bfloat16),
            pltpu.VMEM((k, n2 - 1, ROWS, w), jnp.bfloat16),
            pltpu.SemaphoreType.DMA((k,)),
            pltpu.SemaphoreType.DMA((k, n1 - 1)),
            pltpu.SemaphoreType.DMA((k,)),
            pltpu.SemaphoreType.DMA((k, 1 if self.direct else n2 - 1)),
        ]

    def bind(self, refs):
        (self.s1, self.r1, self.t, self.s2, self.r2, self.ss1, self.rs1, self.ss2, self.rs2) = refs


def groups():
    return [
        Group("y", 0, 512, 4, True),
        Group("z", 512, 768, 4, True),
        Group("y", 1280, 1024, 2, True),
    ]


def shifted(axis, step):
    return lax.rem(lax.axis_index(axis) + step + 2 * SIZE[axis], SIZE[axis])


def remote(src, dst, send, recv, axis, step):
    return pltpu.make_async_remote_copy(
        src_ref=src, dst_ref=dst, send_sem=send, recv_sem=recv,
        device_id={axis: shifted(axis, step)}, device_id_type=MESH,
    )


def kernel(x_ref, enc_ref, eb_ref, dec_ref, db_ref, o_ref, wenc, wdec, ebv, xg, act, part, mvs, mvr, fin, fsend, frecv,
           local_sem, w_ss, w_rs, ay_ss, ay_rs, az_ss, az_rs, bz_ss, bz_rs, by_ss, by_rs, mv_ss, mv_rs, f_ss, f_rs, partner_sem, *rest):
    gs = groups()
    for i, g in enumerate(gs):
        g.bind(rest[9 * i : 9 * i + 9])
    z, y, c, l = (lax.axis_index(a) for a in ("z", "y", "c", "x"))

    locals_ = [
        pltpu.make_async_copy(enc_ref.at[0], wenc.at[c], local_sem.at[0]),
        pltpu.make_async_copy(eb_ref, ebv.at[c], local_sem.at[1]),
        pltpu.make_async_copy(x_ref.at[0], xg.at[y, z], local_sem.at[2]),
    ]
    for cp in locals_:
        cp.start()

    def dec_local(k):
        return pltpu.make_async_copy(dec_ref.at[0, l + k], wdec.at[k, c], local_sem.at[3 + k])

    def dec_push(k):
        return remote(dec_ref.at[0, l + k], wdec.at[k, c], w_ss.at[2 + k], w_rs.at[2 + k], "c", 1)

    def each_k(fn, order=(1, 3, 2, 0)):
        for k in order:
            if k == 0:
                fn(0)
            else:
                pl.when(l + k < X)(lambda k=k: fn(k))

    each_k(lambda k: dec_local(k).start())

    bar = pltpu.get_barrier_semaphore()
    peers = [("y", i) for i in (1, 2, 3)] + [("z", i) for i in range(1, 8)] + [("x", i) for i in (1, 2, 3)]

    @pl.when(c == 0)
    def _():
        pl.semaphore_signal(bar, inc=1, device_id={"c": 1}, device_id_type=MESH)

    for a, i in peers:
        pl.semaphore_signal(bar, inc=1, device_id={a: shifted(a, i)}, device_id_type=MESH)
    pl.semaphore_wait(bar, len(peers) + c)

    @pl.when(c == 1)
    def _():
        pl.semaphore_signal(partner_sem, inc=1, device_id={"c": 0}, device_id_type=MESH)

    lo, hi = pl.ds(0, GATHER_SPLIT), pl.ds(GATHER_SPLIT, D - GATHER_SPLIT)

    def gy(i):
        return remote(x_ref.at[0, :, lo], xg.at[y, z, :, lo], ay_ss.at[0], ay_rs.at[i - 1], "y", i)

    def gz(i):
        return remote(x_ref.at[0, :, hi], xg.at[y, z, :, hi], bz_ss.at[0], bz_rs.at[i - 1], "z", i)

    def along(j, i):
        yb = shifted("y", -j)
        src = x_ref.at[0, :, lo] if j == 0 else xg.at[yb, z, :, lo]
        return remote(src, xg.at[yb, z, :, lo], az_ss.at[0], az_rs.at[i - 1], "z", i)

    far_first = (4, 3, 5, 2, 6, 1, 7)

    def spread_z(j):
        for i in far_first:
            along(j, i).start()

    def across(j, i):
        zb = shifted("z", -j)
        src = x_ref.at[0, :, hi] if j == 0 else xg.at[y, zb, :, hi]
        return remote(src, xg.at[y, zb, :, hi], by_ss.at[0], by_rs.at[i - 1], "y", i)

    def spread(j):
        for i in (1, 3, 2):
            across(j, i).start()

    for i in (1, 3, 2):
        gy(i).start()
    for i in far_first:
        gz(i).start()
    spread(0)
    spread_z(0)

    enc_push = remote(enc_ref.at[0], wenc.at[c], w_ss.at[0], w_rs.at[0], "c", 1)
    eb_push = remote(eb_ref, ebv.at[c], w_ss.at[1], w_rs.at[1], "c", 1)

    def push_weights():
        enc_push.start()
        eb_push.start()
        each_k(lambda k: dec_push(k).start())

    pl.when(c == 1)(push_weights)

    def take_y(i):
        gy(i).wait_recv()
        spread_z(i)

    def take_z(j):
        gz(j).wait_recv()
        spread(j)

    take_z(1), take_z(7), take_y(1), take_y(3), take_z(2), take_z(6), take_y(2), take_z(3), take_z(5), take_z(4)

    @pl.when(c == 0)
    def _():
        pl.semaphore_wait(partner_sem, 1)
        push_weights()

    def all_across(i):
        block = xg.at[y, :, :, hi]
        return remote(block, block, by_ss.at[0], by_rs.at[i - 1], "y", i)

    def all_along(i):
        block = xg.at[:, z, :, lo]
        return remote(block, block, az_ss.at[0], az_rs.at[i - 1], "z", i)

    for i in (1, 3, 2):
        all_across(i).wait_recv()
    for i in (1, 7, 2, 6, 3, 5, 4):
        all_along(i).wait_recv()
    for cp in locals_:
        cp.wait()
    enc_push.wait_recv()
    eb_push.wait_recv()

    rows = xg[...].astype(jnp.float32).reshape(Z * Y * ROWS, D).astype(jnp.bfloat16)
    for side in range(C):
        for n in range(FEATS // TILE):
            at = pl.ds(n * TILE, TILE)
            pre = jnp.dot(rows, wenc[side, :, at], preferred_element_type=jnp.float32) + ebv[side, :, at]
            act[:, pl.ds(side * FEATS + n * TILE, TILE)] = jnp.maximum(pre, 0.0).astype(jnp.bfloat16)

    def product(k, col):
        at = pl.ds(col, TILE)
        weight = wdec[k, :, :, at].reshape(C * FEATS, TILE)
        out = jnp.dot(act[...], weight, preferred_element_type=jnp.float32)
        return out.reshape(Y, Z, ROWS, TILE)

    ready = set()

    def dec_ready(k):
        if k not in ready:
            ready.add(k)
            dec_local(k).wait()
            dec_push(k).wait_recv()

    def move(i, n):
        at = pl.ds(n * TILE, TILE)
        return remote(mvs.at[i, :, :, :, at], mvr.at[i, :, :, :, at], mv_ss.at[i], mv_rs.at[i, n], "x", 1 - 2 * i)

    def moved(k):
        i = k // 2
        dec_ready(k)
        for n in (0, 1, 2, 3):
            mvs[i, :, :, :, pl.ds(n * TILE, TILE)] = product(k, B_COLS + n * TILE).astype(jnp.bfloat16)
            move(i, n).start()

    def own1(g, k, d):
        cols = pl.ds(g.start, g.width)
        return part[k, d, :, :, cols] if g.first == "y" else part[k, :, d, :, cols]

    def own2(g, j, d):
        return g.t[j, d]

    def copy1(g, j, slot, step):
        return remote(g.s1.at[j, slot], g.r1.at[j, slot], g.ss1.at[j], g.rs1.at[j, slot], g.first, step)

    def copy2(g, j, slot, step):
        return remote(g.s2.at[j, slot], g.r2.at[j, slot], g.ss2.at[j], g.rs2.at[j, 0 if g.direct else slot], g.second, step)

    def stage_of(g, stage, j, k):
        if stage == 1:
            return g.first, g.n1, (lambda d: own1(g, k, d)), g.s1, g.r1, (lambda slot, step: copy1(g, j, slot, step))
        return g.second, g.n2, (lambda d: own2(g, j, d)), g.s2, g.r2, (lambda slot, step: copy2(g, j, slot, step))

    done = {}

    def chain_step(i, stage, k, long, s):
        g = gs[i]
        j = k if g.ks == X else k // 2
        axis, size, own, sref, rref, copy = stage_of(g, stage, j, k)
        half = size // 2
        hops, base = (half, 0) if long else (half - 1, half)
        step = (1 if j % 2 == 0 else -1) * (1 if long else -1)
        if s > 0:
            copy(base + s - 1, step).wait_recv()
        if s < hops:
            msg = own(shifted(axis, step * (hops - s)))
            if s > 0:
                msg = msg + rref[j, base + s - 1].astype(jnp.float32)
            sref[j, base + s] = msg.astype(jnp.bfloat16)
            copy(base + s, step).start()
            return
        done[i, stage, k] = done.get((i, stage, k), 0) + 1
        if done[i, stage, k] == 2:
            total = own(lax.axis_index(axis)) + rref[j, half - 1].astype(jnp.float32) + rref[j, size - 2].astype(jnp.float32)
            if stage == 2:
                fin[k, :, pl.ds(g.start, g.width)] = total
                return
            g.t[j] = total
            if g.direct:
                direct_send(g, j)
            else:
                begin(i, 2, k)

    def begin(i, stage, k):
        chain_step(i, stage, k, True, 0)
        chain_step(i, stage, k, False, 0)

    def direct_send(g, j):
        for o in sorted(range(1, g.n2), key=lambda o: -min(o, g.n2 - o)):
            g.s2[j, o - 1] = own2(g, j, shifted(g.second, o)).astype(jnp.bfloat16)
            copy2(g, j, o - 1, o).start()

    def direct_sum(i, k):
        g = gs[i]
        j = k if g.ks == X else k // 2
        remote(g.s2.at[j], g.r2.at[j], g.ss2.at[j], g.rs2.at[j, 0], g.second, 1).wait_recv()
        total = own2(g, j, lax.axis_index(g.second))
        for o in range(1, g.n2):
            total = total + g.r2[j, o - 1].astype(jnp.float32)
        fin[k, :, pl.ds(g.start, g.width)] = total

    def low_columns(k):
        dec_ready(k)
        for n in range(B_COLS // TILE):
            part[k, :, :, :, pl.ds(n * TILE, TILE)] = product(k, n * TILE)
        begin(0, 1, k)
        begin(1, 1, k)

    def high_columns(k):
        dec_ready(k)
        for n in range(A_COLS // TILE):
            at = B_COLS + n * TILE
            part[k, :, :, :, pl.ds(at, TILE)] = product(k, at)
        if k:
            begin(2, 1, k)

    def join(i, n):
        move(i, n).wait_recv()
        at = pl.ds(B_COLS + n * TILE, TILE)
        part[0, :, :, :, at] = part[0, :, :, :, at] + mvr[i, :, :, :, pl.ds(n * TILE, TILE)].astype(jnp.float32)

    def own_target(i):
        tiles = range((gs[i].start - B_COLS) // TILE, (gs[i].start - B_COLS + gs[i].width) // TILE)
        pl.when(l > 0)(lambda: [join(0, n) for n in tiles] and None)
        pl.when(l == X - 1)(lambda: [join(1, n) for n in tiles] and None)
        begin(i, 1, 0)

    def late(k, is_a):
        at = pl.ds(B_COLS, A_COLS) if is_a else pl.ds(0, B_COLS)
        slot = 3 if is_a else k - 1
        return remote(fsend.at[k - 1, :, at], frecv.at[k - 1, :, at], f_ss.at[slot], f_rs.at[slot], "x", k)

    def send_late(k, is_a):
        at = pl.ds(B_COLS, A_COLS) if is_a else pl.ds(0, B_COLS)
        fsend[k - 1, :, at] = fin[k, :, at].astype(jnp.bfloat16)
        late(k, is_a).start()

    left = {(k, is_a): 1 if is_a else 2 for k in range(X) for is_a in (False, True)}

    def run(kind, *rest):
        k = rest[2] if kind == 4 else rest[1] if kind == 5 else 0 if kind == 3 else rest[0]

        def act_():
            if kind == 0:
                low_columns(k)
            elif kind == 1:
                moved(k)
            elif kind == 2:
                high_columns(k)
            elif kind == 3:
                own_target(rest[0])
            else:
                if kind == 4:
                    chain_step(*rest)
                else:
                    direct_sum(*rest)
                i = rest[0]
                last = kind == 5 or (rest[1] == 2 and done.get((i, 2, k), 0) == 2)
                if last:
                    left[k, i >= 2] -= 1
                    if k and not left[k, i >= 2]:
                        send_late(k, i >= 2)

        if k == 0:
            act_()
        else:
            pl.when(l + k < X)(act_)

    for step in ORDER:
        run(*step)

    def take_late(k, is_a):
        late(k, is_a).wait_recv()
        at = pl.ds(B_COLS, A_COLS) if is_a else pl.ds(0, B_COLS)
        fin[0, :, at] = fin[0, :, at] + frecv[k - 1, :, at].astype(jnp.float32)

    for k in (1, 2, 3):
        pl.when(l >= k)(lambda k=k: take_late(k, False))
    pl.when(l >= 2)(lambda: take_late(2, True))
    o_ref[0] = (fin[0] + db_ref[...]).astype(jnp.bfloat16)

    def left_all(src, send, recv):
        remote(src, src, send, recv, "y", 1).wait_send()

    left_all(xg.at[0, pl.ds(0, 3), :, lo], ay_ss.at[0], ay_rs.at[0])
    left_all(xg.at[:, pl.ds(0, 7), :, lo], az_ss.at[0], az_rs.at[0])
    left_all(xg.at[0, pl.ds(0, 7), :, hi], bz_ss.at[0], bz_rs.at[0])
    left_all(xg.at[pl.ds(0, 3), :, :, hi], by_ss.at[0], by_rs.at[0])
    enc_push.wait_send()
    eb_push.wait_send()
    each_k(lambda k: dec_push(k).wait_send())
    each_k(lambda k: left_all(mvs.at[k // 2], mv_ss.at[k // 2], mv_rs.at[k // 2, 0]), (1, 3))
    each_k(lambda k: late(k, False).wait_send(), (1, 2, 3))
    pl.when(l < 2)(lambda: late(2, True).wait_send())

    def drain(g, j):
        left_all(g.s1.at[j], g.ss1.at[j], g.rs1.at[j, 0])
        left_all(g.s2.at[j], g.ss2.at[j], g.rs2.at[j, 0])

    each_k(lambda k: [drain(g, k if g.ks == X else k // 2) for g in gs if g.ks == X or k % 2 == 0] and None)


def per_device(resid_in, enc_weight, enc_bias, dec_weight, dec_bias):
    dma = pltpu.SemaphoreType.DMA
    scratch = [
        pltpu.VMEM((C, D, FEATS), jnp.bfloat16),
        pltpu.VMEM((X, C, FEATS, D), jnp.bfloat16),
        pltpu.VMEM((C, 1, FEATS), jnp.float32),
        pltpu.VMEM((Y, Z, ROWS, D), jnp.bfloat16),
        pltpu.VMEM((Z * Y * ROWS, C * FEATS), jnp.bfloat16),
        pltpu.VMEM((X, Y, Z, ROWS, D), jnp.float32),
        pltpu.VMEM((2, Y, Z, ROWS, A_COLS), jnp.bfloat16),
        pltpu.VMEM((2, Y, Z, ROWS, A_COLS), jnp.bfloat16),
        pltpu.VMEM((X, ROWS, D), jnp.float32),
        pltpu.VMEM((X - 1, ROWS, D), jnp.bfloat16),
        pltpu.VMEM((X - 1, ROWS, D), jnp.bfloat16),
        dma((7,)),
        dma((6,)), dma((6,)),
        dma((1,)), dma((3,)),
        dma((1,)), dma((7,)),
        dma((1,)), dma((7,)),
        dma((1,)), dma((3,)),
        dma((2,)), dma((2, A_COLS // TILE)),
        dma((4,)), dma((4,)),
        pltpu.SemaphoreType.REGULAR,
    ]
    for g in groups():
        scratch += g.scratch()
    anywhere = pl.BlockSpec(memory_space=pl.ANY)
    return pl.pallas_call(
        kernel,
        out_shape=jax.ShapeDtypeStruct((1, ROWS, D), jnp.bfloat16),
        in_specs=[anywhere, anywhere, anywhere, anywhere, pl.BlockSpec(memory_space=pltpu.VMEM)],
        out_specs=pl.BlockSpec(memory_space=pltpu.VMEM),
        scratch_shapes=scratch,
        compiler_params=pltpu.CompilerParams(collective_id=0, has_side_effects=True, vmem_limit_bytes=67043328),
        name="transcoder",
    )(resid_in, enc_weight, enc_bias, dec_weight, dec_bias)


def solution(mesh):
    finer = Mesh(mesh.devices.reshape(Z, Y, C, X), ("z", "y", "c", "x"))
    return jax.shard_map(
        per_device,
        mesh=finer,
        in_specs=(
            P("x", FEAT, None),
            P("x", None, FEAT),
            P("x", FEAT),
            P("x", None, FEAT, None),
            P("x", None),
        ),
        out_specs=P("x", FEAT, None),
        check_vma=False,
    )
```

```python
import jax
import jax.numpy as jnp
from jax import lax
from jax.experimental import pallas as pl
from jax.experimental.pallas import tpu as pltpu
from jax.sharding import Mesh
from jax.sharding import PartitionSpec as P

FEAT = ("z", "y", "c")
MESH = pl.DeviceIdType.MESH
Z, Y, C, X = 8, 4, 2, 4
SIZE = {"z": Z, "y": Y, "c": C, "x": X}
ROWS = 8
D = 2304
FEATS = 512
TILE = 256
GATHER_SPLIT = 768
B_COLS = 1280
A_COLS = D - B_COLS

ORDER = (
    (1,1), (1,3), (0,1), (0,2), (2,2), (0,3), (0,0), (4,1,1,1,1,1), (4,1,1,1,0,1), (4,0,1,1,1,1), (4,0,1,1,0,1), (2,0), (4,1,1,2,1,1),
    (4,1,1,2,0,1), (4,0,1,2,1,1), (4,0,1,2,0,1), (4,1,1,3,1,1), (4,1,1,3,0,1), (4,1,1,0,1,1), (4,1,1,0,0,1), (4,2,1,2,1,1),
    (4,2,1,2,0,1), (4,1,1,1,1,2), (4,1,1,1,0,2), (4,1,1,2,1,2), (4,1,1,2,0,2), (4,0,1,3,1,1), (4,0,1,3,0,1), (4,1,1,3,1,2),
    (4,1,1,3,0,2), (3,2), (4,0,1,0,1,1), (4,0,1,0,0,1), (4,1,1,0,1,2), (4,1,1,0,0,2), (4,0,1,1,1,2), (4,0,1,2,1,2), (4,1,1,1,1,3),
    (4,1,1,1,0,3), (4,1,1,2,1,3), (4,1,1,2,0,3), (4,1,1,3,1,3), (4,1,1,3,0,3), (4,2,1,2,1,2), (4,1,1,0,1,3), (4,1,1,0,0,3),
    (4,2,1,0,1,1), (4,0,1,3,1,2), (4,0,1,0,1,2), (5,0,1), (4,2,1,0,0,1), (4,1,1,1,1,4), (4,1,1,2,1,4), (5,0,2), (4,1,1,3,1,4),
    (4,2,1,0,1,2), (4,1,1,0,1,4), (5,1,1), (5,1,2), (5,1,3), (5,2,2), (5,1,0), (5,0,3), (5,0,0), (5,2,0),
)

class Group:
    def __init__(self, first, start, width, ks, direct):
        self.first, self.second = first, "y" if first == "z" else "z"
        self.start, self.width, self.ks = start, width, ks
        self.n1, self.n2 = SIZE[self.first], SIZE[self.second]
        self.direct = direct

    def scratch(self):
        k, n1, n2, w = self.ks, self.n1, self.n2, self.width
        return [
            pltpu.VMEM((k, n1 - 1, n2, ROWS, w), jnp.bfloat16),
            pltpu.VMEM((k, n1 - 1, n2, ROWS, w), jnp.bfloat16),
            pltpu.VMEM((k, n2, ROWS, w), jnp.float32),
            pltpu.VMEM((k, n2 - 1, ROWS, w), jnp.bfloat16),
            pltpu.VMEM((k, n2 - 1, ROWS, w), jnp.bfloat16),
            pltpu.SemaphoreType.DMA((k,)),
            pltpu.SemaphoreType.DMA((k, n1 - 1)),
            pltpu.SemaphoreType.DMA((k,)),
            pltpu.SemaphoreType.DMA((k, 1 if self.direct else n2 - 1)),
        ]

    def bind(self, refs):
        (self.s1, self.r1, self.t, self.s2, self.r2, self.ss1, self.rs1, self.ss2, self.rs2) = refs


def groups():
    return [
        Group("y", 0, 512, 4, True),
        Group("z", 512, 768, 4, True),
        Group("y", 1280, 1024, 2, True),
    ]


def shifted(axis, step):
    return lax.rem(lax.axis_index(axis) + step + 2 * SIZE[axis], SIZE[axis])


def remote(src, dst, send, recv, axis, step):
    return pltpu.make_async_remote_copy(
        src_ref=src, dst_ref=dst, send_sem=send, recv_sem=recv,
        device_id={axis: shifted(axis, step)}, device_id_type=MESH,
    )


def kernel(x_ref, enc_ref, eb_ref, dec_ref, db_ref, o_ref, wenc, wdec, ebv, xg, act, part, mvs, mvr, fin, fsend, frecv,
           local_sem, w_ss, w_rs, ay_ss, ay_rs, az_ss, az_rs, bz_ss, bz_rs, by_ss, by_rs, mv_ss, mv_rs, f_ss, f_rs, partner_sem, *rest):
    gs = groups()
    for i, g in enumerate(gs):
        g.bind(rest[9 * i : 9 * i + 9])
    z, y, c, l = (lax.axis_index(a) for a in ("z", "y", "c", "x"))

    locals_ = [
        pltpu.make_async_copy(enc_ref.at[0], wenc.at[c], local_sem.at[0]),
        pltpu.make_async_copy(eb_ref, ebv.at[c], local_sem.at[1]),
        pltpu.make_async_copy(x_ref.at[0], xg.at[y, z], local_sem.at[2]),
    ]
    for cp in locals_:
        cp.start()

    def dec_local(k):
        return pltpu.make_async_copy(dec_ref.at[0, l + k], wdec.at[k, c], local_sem.at[3 + k])

    def dec_push(k):
        return remote(dec_ref.at[0, l + k], wdec.at[k, c], w_ss.at[2 + k], w_rs.at[2 + k], "c", 1)

    def each_k(fn, order=(1, 3, 2, 0)):
        for k in order:
            if k == 0:
                fn(0)
            else:
                pl.when(l + k < X)(lambda k=k: fn(k))

    each_k(lambda k: dec_local(k).start())

    bar = pltpu.get_barrier_semaphore()
    peers = [("y", i) for i in (1, 2, 3)] + [("z", i) for i in (1, 2, 6, 7)] + [("x", i) for i in (1, 2, 3)]

    @pl.when(c == 0)
    def _():
        pl.semaphore_signal(bar, inc=1, device_id={"c": 1}, device_id_type=MESH)

    for a, i in peers:
        pl.semaphore_signal(bar, inc=1, device_id={a: shifted(a, i)}, device_id_type=MESH)
    pl.semaphore_wait(bar, len(peers) + c)

    @pl.when(c == 1)
    def _():
        pl.semaphore_signal(partner_sem, inc=1, device_id={"c": 0}, device_id_type=MESH)

    lo, hi = pl.ds(0, GATHER_SPLIT), pl.ds(GATHER_SPLIT, D - GATHER_SPLIT)

    def gy(i):
        return remote(x_ref.at[0, :, lo], xg.at[y, z, :, lo], ay_ss.at[0], ay_rs.at[i - 1], "y", i)

    def high(off, step):
        zb = shifted("z", -off)
        at = lax.rem(off + step + 2 * Z, Z) - 1
        return remote(xg.at[y, zb, :, hi], xg.at[y, zb, :, hi], bz_ss.at[0], bz_rs.at[at], "z", step)

    def own_high(step):
        return remote(x_ref.at[0, :, hi], xg.at[y, z, :, hi], bz_ss.at[0], bz_rs.at[step % Z - 1], "z", step)

    def low(j, off, step):
        yb, zb = shifted("y", -j), shifted("z", -off)
        src = x_ref.at[0, :, lo] if j == 0 and off == 0 else xg.at[yb, zb, :, lo]
        to = (off + step) % Z
        at = 7 + (to == 6) * 4 + j if to in (2, 6) else to - 1
        return remote(src, xg.at[yb, zb, :, lo], az_ss.at[0], az_rs.at[at], "z", step)

    def spread_z(j):
        for step in (2, -2, 1, -1):
            low(j, 0, step).start()

    def relay_low(j):
        for sign in (1, -1):
            low(j, 0, 2 * sign).wait_recv()
            long = sign == (1 if j % 2 == 0 else -1)
            for step in (2, 1) if long else (1,):
                low(j, 2 * sign, step * sign).start()

    def across(j, i):
        zb = shifted("z", -j)
        src = x_ref.at[0, :, hi] if j == 0 else xg.at[y, zb, :, hi]
        return remote(src, xg.at[y, zb, :, hi], by_ss.at[0], by_rs.at[i - 1], "y", i)

    def spread(j):
        for i in (1, 3, 2):
            across(j, i).start()

    for i in (1, 3, 2):
        gy(i).start()
    for step in (2, -2, 1, -1):
        own_high(step).start()
    spread(0)
    spread_z(0)

    enc_push = remote(enc_ref.at[0], wenc.at[c], w_ss.at[0], w_rs.at[0], "c", 1)
    eb_push = remote(eb_ref, ebv.at[c], w_ss.at[1], w_rs.at[1], "c", 1)

    def push_weights():
        enc_push.start()
        eb_push.start()
        each_k(lambda k: dec_push(k).start())

    @pl.when(c == 0)
    def _():
        pl.semaphore_wait(partner_sem, 1)

    push_weights()

    def take_y(i):
        gy(i).wait_recv()
        spread_z(i)

    turn = 1 - 2 * lax.rem(y, 2)

    def take_z(off):
        own_high(off).wait_recv()
        spread(off)

    def relay_z(off):
        own_high(off).wait_recv()
        sign = 1 if off == 2 else -1
        high(2 * sign, sign).start()

        @pl.when(turn == sign)
        def _():
            high(2 * sign, 2 * sign).start()

        spread(off)

    take_z(1), take_z(7), take_y(1), take_y(3), relay_z(2), relay_z(6), relay_low(0), take_y(2), relay_low(1), relay_low(3)
    take_z(3), take_z(5), take_z(4), relay_low(2)

    def all_across(i):
        block = xg.at[y, :, :, hi]
        return remote(block, block, by_ss.at[0], by_rs.at[i - 1], "y", i)

    def all_along(i):
        block = xg.at[:, z, :, lo]
        return remote(block, block, az_ss.at[0], az_rs.at[i - 1], "z", i)

    for i in (1, 3, 2):
        all_across(i).wait_recv()
    for i in (1, 7, 3, 5, 4):
        all_along(i).wait_recv()
    for cp in locals_:
        cp.wait()
    enc_push.wait_recv()
    eb_push.wait_recv()

    rows = xg[...].astype(jnp.float32).reshape(Z * Y * ROWS, D).astype(jnp.bfloat16)
    for side in range(C):
        for n in range(FEATS // TILE):
            at = pl.ds(n * TILE, TILE)
            pre = jnp.dot(rows, wenc[side, :, at], preferred_element_type=jnp.float32) + ebv[side, :, at]
            act[:, pl.ds(side * FEATS + n * TILE, TILE)] = jnp.maximum(pre, 0.0).astype(jnp.bfloat16)

    def product(k, col):
        at = pl.ds(col, TILE)
        weight = wdec[k, :, :, at].reshape(C * FEATS, TILE)
        out = jnp.dot(act[...], weight, preferred_element_type=jnp.float32)
        return out.reshape(Y, Z, ROWS, TILE)

    ready = set()

    def dec_ready(k):
        if k not in ready:
            ready.add(k)
            dec_local(k).wait()
            dec_push(k).wait_recv()

    def move(i, n):
        at = pl.ds(n * TILE, TILE)
        return remote(mvs.at[i, :, :, :, at], mvr.at[i, :, :, :, at], mv_ss.at[i], mv_rs.at[i, n], "x", 1 - 2 * i)

    def moved(k):
        i = k // 2
        dec_ready(k)
        for n in (0, 1, 2, 3):
            mvs[i, :, :, :, pl.ds(n * TILE, TILE)] = product(k, B_COLS + n * TILE).astype(jnp.bfloat16)
            move(i, n).start()

    def own1(g, k, d):
        cols = pl.ds(g.start, g.width)
        return part[k, d, :, :, cols] if g.first == "y" else part[k, :, d, :, cols]

    def own2(g, j, d):
        return g.t[j, d]

    def copy1(g, j, slot, step):
        return remote(g.s1.at[j, slot], g.r1.at[j, slot], g.ss1.at[j], g.rs1.at[j, slot], g.first, step)

    def copy2(g, j, slot, step):
        return remote(g.s2.at[j, slot], g.r2.at[j, slot], g.ss2.at[j], g.rs2.at[j, 0 if g.direct else slot], g.second, step)

    def stage_of(g, stage, j, k):
        if stage == 1:
            return g.first, g.n1, (lambda d: own1(g, k, d)), g.s1, g.r1, (lambda slot, step: copy1(g, j, slot, step))
        return g.second, g.n2, (lambda d: own2(g, j, d)), g.s2, g.r2, (lambda slot, step: copy2(g, j, slot, step))

    done = {}

    def chain_step(i, stage, k, long, s):
        g = gs[i]
        j = k if g.ks == X else k // 2
        axis, size, own, sref, rref, copy = stage_of(g, stage, j, k)
        half = size // 2
        hops, base = (half, 0) if long else (half - 1, half)
        step = (1 if j % 2 == 0 else -1) * (1 if long else -1)
        if s > 0:
            copy(base + s - 1, step).wait_recv()
        if s < hops:
            msg = own(shifted(axis, step * (hops - s)))
            if s > 0:
                msg = msg + rref[j, base + s - 1].astype(jnp.float32)
            sref[j, base + s] = msg.astype(jnp.bfloat16)
            copy(base + s, step).start()
            return
        done[i, stage, k] = done.get((i, stage, k), 0) + 1
        if done[i, stage, k] == 2:
            total = own(lax.axis_index(axis)) + rref[j, half - 1].astype(jnp.float32) + rref[j, size - 2].astype(jnp.float32)
            if stage == 2:
                fin[k, :, pl.ds(g.start, g.width)] = total
                return
            g.t[j] = total
            if g.direct:
                direct_send(g, j)
            else:
                begin(i, 2, k)

    def begin(i, stage, k):
        chain_step(i, stage, k, True, 0)
        chain_step(i, stage, k, False, 0)

    def direct_send(g, j):
        for o in sorted(range(1, g.n2), key=lambda o: -min(o, g.n2 - o)):
            g.s2[j, o - 1] = own2(g, j, shifted(g.second, o)).astype(jnp.bfloat16)
            copy2(g, j, o - 1, o).start()

    def direct_sum(i, k):
        g = gs[i]
        j = k if g.ks == X else k // 2
        remote(g.s2.at[j], g.r2.at[j], g.ss2.at[j], g.rs2.at[j, 0], g.second, 1).wait_recv()
        total = own2(g, j, lax.axis_index(g.second))
        for o in range(1, g.n2):
            total = total + g.r2[j, o - 1].astype(jnp.float32)
        fin[k, :, pl.ds(g.start, g.width)] = total

    def low_columns(k):
        dec_ready(k)
        for n in range(B_COLS // TILE):
            part[k, :, :, :, pl.ds(n * TILE, TILE)] = product(k, n * TILE)
        begin(0, 1, k)
        begin(1, 1, k)

    def high_columns(k):
        dec_ready(k)
        for n in range(A_COLS // TILE):
            at = B_COLS + n * TILE
            part[k, :, :, :, pl.ds(at, TILE)] = product(k, at)
        if k:
            begin(2, 1, k)

    def join(i, n):
        move(i, n).wait_recv()
        at = pl.ds(B_COLS + n * TILE, TILE)
        part[0, :, :, :, at] = part[0, :, :, :, at] + mvr[i, :, :, :, pl.ds(n * TILE, TILE)].astype(jnp.float32)

    def own_target(i):
        tiles = range((gs[i].start - B_COLS) // TILE, (gs[i].start - B_COLS + gs[i].width) // TILE)
        pl.when(l > 0)(lambda: [join(0, n) for n in tiles] and None)
        pl.when(l == X - 1)(lambda: [join(1, n) for n in tiles] and None)
        begin(i, 1, 0)

    def late(k, is_a):
        at = pl.ds(B_COLS, A_COLS) if is_a else pl.ds(0, B_COLS)
        slot = 3 if is_a else k - 1
        return remote(fsend.at[k - 1, :, at], frecv.at[k - 1, :, at], f_ss.at[slot], f_rs.at[slot], "x", k)

    def send_late(k, is_a):
        at = pl.ds(B_COLS, A_COLS) if is_a else pl.ds(0, B_COLS)
        fsend[k - 1, :, at] = fin[k, :, at].astype(jnp.bfloat16)
        late(k, is_a).start()

    left = {(k, is_a): 1 if is_a else 2 for k in range(X) for is_a in (False, True)}

    def run(kind, *rest):
        k = rest[2] if kind == 4 else rest[1] if kind == 5 else 0 if kind == 3 else rest[0]

        def act_():
            if kind == 0:
                low_columns(k)
            elif kind == 1:
                moved(k)
            elif kind == 2:
                high_columns(k)
            elif kind == 3:
                own_target(rest[0])
            else:
                if kind == 4:
                    chain_step(*rest)
                else:
                    direct_sum(*rest)
                i = rest[0]
                last = kind == 5 or (rest[1] == 2 and done.get((i, 2, k), 0) == 2)
                if last:
                    left[k, i >= 2] -= 1
                    if k and not left[k, i >= 2]:
                        send_late(k, i >= 2)

        if k == 0:
            act_()
        else:
            pl.when(l + k < X)(act_)

    for step in ORDER:
        run(*step)

    def take_late(k, is_a):
        late(k, is_a).wait_recv()
        at = pl.ds(B_COLS, A_COLS) if is_a else pl.ds(0, B_COLS)
        fin[0, :, at] = fin[0, :, at] + frecv[k - 1, :, at].astype(jnp.float32)

    for k in (1, 2, 3):
        pl.when(l >= k)(lambda k=k: take_late(k, False))
    pl.when(l >= 2)(lambda: take_late(2, True))
    o_ref[0] = (fin[0] + db_ref[...]).astype(jnp.bfloat16)

    def left_all(src, send, recv):
        remote(src, src, send, recv, "y", 1).wait_send()

    left_all(xg.at[0, pl.ds(0, 3), :, lo], ay_ss.at[0], ay_rs.at[0])
    left_all(xg.at[:, pl.ds(0, 7), :, lo], az_ss.at[0], az_rs.at[0])
    left_all(xg.at[0, pl.ds(0, 7), :, hi], bz_ss.at[0], bz_rs.at[0])
    left_all(xg.at[pl.ds(0, 3), :, :, hi], by_ss.at[0], by_rs.at[0])
    enc_push.wait_send()
    eb_push.wait_send()
    each_k(lambda k: dec_push(k).wait_send())
    each_k(lambda k: left_all(mvs.at[k // 2], mv_ss.at[k // 2], mv_rs.at[k // 2, 0]), (1, 3))
    each_k(lambda k: late(k, False).wait_send(), (1, 2, 3))
    pl.when(l < 2)(lambda: late(2, True).wait_send())

    def drain(g, j):
        left_all(g.s1.at[j], g.ss1.at[j], g.rs1.at[j, 0])
        left_all(g.s2.at[j], g.ss2.at[j], g.rs2.at[j, 0])

    each_k(lambda k: [drain(g, k if g.ks == X else k // 2) for g in gs if g.ks == X or k % 2 == 0] and None)


def per_device(resid_in, enc_weight, enc_bias, dec_weight, dec_bias):
    dma = pltpu.SemaphoreType.DMA
    scratch = [
        pltpu.VMEM((C, D, FEATS), jnp.bfloat16),
        pltpu.VMEM((X, C, FEATS, D), jnp.bfloat16),
        pltpu.VMEM((C, 1, FEATS), jnp.float32),
        pltpu.VMEM((Y, Z, ROWS, D), jnp.bfloat16),
        pltpu.VMEM((Z * Y * ROWS, C * FEATS), jnp.bfloat16),
        pltpu.VMEM((X, Y, Z, ROWS, D), jnp.float32),
        pltpu.VMEM((2, Y, Z, ROWS, A_COLS), jnp.bfloat16),
        pltpu.VMEM((2, Y, Z, ROWS, A_COLS), jnp.bfloat16),
        pltpu.VMEM((X, ROWS, D), jnp.float32),
        pltpu.VMEM((X - 1, ROWS, D), jnp.bfloat16),
        pltpu.VMEM((X - 1, ROWS, D), jnp.bfloat16),
        dma((7,)),
        dma((6,)), dma((6,)),
        dma((1,)), dma((3,)),
        dma((1,)), dma((15,)),
        dma((1,)), dma((7,)),
        dma((1,)), dma((3,)),
        dma((2,)), dma((2, A_COLS // TILE)),
        dma((4,)), dma((4,)),
        pltpu.SemaphoreType.REGULAR,
    ]
    for g in groups():
        scratch += g.scratch()
    anywhere = pl.BlockSpec(memory_space=pl.ANY)
    return pl.pallas_call(
        kernel,
        out_shape=jax.ShapeDtypeStruct((1, ROWS, D), jnp.bfloat16),
        in_specs=[anywhere, anywhere, anywhere, anywhere, pl.BlockSpec(memory_space=pltpu.VMEM)],
        out_specs=pl.BlockSpec(memory_space=pltpu.VMEM),
        scratch_shapes=scratch,
        compiler_params=pltpu.CompilerParams(collective_id=0, has_side_effects=True, vmem_limit_bytes=67043328),
        name="transcoder",
    )(resid_in, enc_weight, enc_bias, dec_weight, dec_bias)


def solution(mesh):
    finer = Mesh(mesh.devices.reshape(Z, Y, C, X), ("z", "y", "c", "x"))
    return jax.shard_map(
        per_device,
        mesh=finer,
        in_specs=(
            P("x", FEAT, None),
            P("x", None, FEAT),
            P("x", FEAT),
            P("x", None, FEAT, None),
            P("x", None),
        ),
        out_specs=P("x", FEAT, None),
        check_vma=False,
    )
```

```python
import jax
import jax.numpy as jnp
from jax import lax
from jax.experimental import pallas as pl
from jax.experimental.pallas import tpu as pltpu
from jax.sharding import Mesh
from jax.sharding import PartitionSpec as P

FEAT = ("z", "y", "c")
MESH = pl.DeviceIdType.MESH
Z, Y, C, X = 8, 4, 2, 4
SIZE = {"z": Z, "y": Y, "c": C, "x": X}
ROWS = 8
D = 2304
FEATS = 512
TILE = 256
GATHER_SPLIT = 768
B_COLS = 1280
A_COLS = D - B_COLS

ORDER = (
    (0,1), (1,1), (1,3), (4,1,1,1,1,1), (4,1,1,1,0,1), (4,0,1,1,1,1), (4,0,1,1,0,1), (0,3), (0,2), (2,2), (4,1,1,1,1,2),
    (4,1,1,1,0,2), (0,0), (4,0,1,1,1,2), (4,1,1,3,1,1), (4,1,1,3,0,1), (2,0), (4,0,1,3,0,1), (4,0,1,3,1,1), (4,1,1,2,1,1),
    (4,1,1,2,0,1), (4,0,1,2,1,1), (4,0,1,2,0,1), (4,1,1,1,1,3), (4,1,1,1,0,3), (4,1,1,0,1,1), (4,1,1,0,0,1), (4,2,1,2,0,1),
    (4,2,1,2,1,1), (4,1,1,3,0,2), (3,2), (4,0,1,0,1,1), (4,1,1,3,1,2), (4,0,1,0,0,1), (4,1,1,2,1,2), (5,0,1), (4,1,1,2,0,2),
    (4,0,1,2,1,2), (4,1,1,0,1,2), (4,0,1,3,1,2), (4,1,1,1,1,4), (4,1,1,3,0,3), (4,1,1,0,0,2), (4,1,1,2,1,3), (4,1,1,3,1,3),
    (4,2,1,2,1,2), (4,2,1,0,1,1), (4,1,1,2,0,3), (4,0,1,0,1,2), (4,1,1,0,1,3), (4,2,1,0,0,1), (5,0,2), (4,1,1,2,1,4), (5,1,1),
    (4,1,1,0,0,3), (5,0,3), (4,2,1,0,1,2), (4,1,1,3,1,4), (5,1,2), (4,1,1,0,1,4), (5,1,3), (5,2,2), (5,0,0), (5,1,0), (5,2,0),
)

class Group:
    def __init__(self, first, start, width, ks, direct):
        self.first, self.second = first, "y" if first == "z" else "z"
        self.start, self.width, self.ks = start, width, ks
        self.n1, self.n2 = SIZE[self.first], SIZE[self.second]
        self.direct = direct

    def scratch(self):
        k, n1, n2, w = self.ks, self.n1, self.n2, self.width
        return [
            pltpu.VMEM((k, n1 - 1, n2, ROWS, w), jnp.bfloat16),
            pltpu.VMEM((k, n1 - 1, n2, ROWS, w), jnp.bfloat16),
            pltpu.VMEM((k, n2, ROWS, w), jnp.float32),
            pltpu.VMEM((k, n2 - 1, ROWS, w), jnp.bfloat16),
            pltpu.VMEM((k, n2 - 1, ROWS, w), jnp.bfloat16),
            pltpu.SemaphoreType.DMA((k,)),
            pltpu.SemaphoreType.DMA((k, n1 - 1)),
            pltpu.SemaphoreType.DMA((k,)),
            pltpu.SemaphoreType.DMA((k, 1 if self.direct else n2 - 1)),
        ]

    def bind(self, refs):
        (self.s1, self.r1, self.t, self.s2, self.r2, self.ss1, self.rs1, self.ss2, self.rs2) = refs


def groups():
    return [
        Group("y", 0, 512, 4, True),
        Group("z", 512, 768, 4, True),
        Group("y", 1280, 1024, 2, True),
    ]


def shifted(axis, step):
    return lax.rem(lax.axis_index(axis) + step + 2 * SIZE[axis], SIZE[axis])


def remote(src, dst, send, recv, axis, step):
    return pltpu.make_async_remote_copy(
        src_ref=src, dst_ref=dst, send_sem=send, recv_sem=recv,
        device_id={axis: shifted(axis, step)}, device_id_type=MESH,
    )


def kernel(x_ref, enc_ref, eb_ref, dec_ref, db_ref, o_ref, wenc, wdec, ebv, xg, act, part, mvs, mvr, fin, fsend, frecv,
           local_sem, w_ss, w_rs, ay_ss, ay_rs, az_ss, az_rs, bz_ss, bz_rs, by_ss, by_rs, mv_ss, mv_rs, f_ss, f_rs, partner_sem, *rest):
    gs = groups()
    for i, g in enumerate(gs):
        g.bind(rest[9 * i : 9 * i + 9])
    z, y, c, l = (lax.axis_index(a) for a in ("z", "y", "c", "x"))

    locals_ = [
        pltpu.make_async_copy(enc_ref.at[0], wenc.at[c], local_sem.at[0]),
        pltpu.make_async_copy(eb_ref, ebv.at[c], local_sem.at[1]),
        pltpu.make_async_copy(x_ref.at[0], xg.at[y, z], local_sem.at[2]),
    ]
    for cp in locals_:
        cp.start()

    def dec_local(k):
        return pltpu.make_async_copy(dec_ref.at[0, l + k], wdec.at[k, c], local_sem.at[3 + k])

    def dec_push(k):
        return remote(dec_ref.at[0, l + k], wdec.at[k, c], w_ss.at[2 + k], w_rs.at[2 + k], "c", 1)

    def each_k(fn, order=(1, 3, 2, 0)):
        for k in order:
            if k == 0:
                fn(0)
            else:
                pl.when(l + k < X)(lambda k=k: fn(k))

    each_k(lambda k: dec_local(k).start())

    bar = pltpu.get_barrier_semaphore()
    peers = [("y", i) for i in (1, 2, 3)] + [("z", i) for i in (1, 2, 6, 7)] + [("x", i) for i in (1, 2, 3)]

    @pl.when(c == 0)
    def _():
        pl.semaphore_signal(bar, inc=1, device_id={"c": 1}, device_id_type=MESH)

    for a, i in peers:
        pl.semaphore_signal(bar, inc=1, device_id={a: shifted(a, i)}, device_id_type=MESH)
    pl.semaphore_wait(bar, len(peers) + c)

    @pl.when(c == 1)
    def _():
        pl.semaphore_signal(partner_sem, inc=1, device_id={"c": 0}, device_id_type=MESH)

    lo, hi = pl.ds(0, GATHER_SPLIT), pl.ds(GATHER_SPLIT, D - GATHER_SPLIT)

    def gy(i):
        return remote(x_ref.at[0, :, lo], xg.at[y, z, :, lo], ay_ss.at[0], ay_rs.at[i - 1], "y", i)

    def high(off, step):
        zb = shifted("z", -off)
        at = lax.rem(off + step + 2 * Z, Z) - 1
        return remote(xg.at[y, zb, :, hi], xg.at[y, zb, :, hi], bz_ss.at[0], bz_rs.at[at], "z", step)

    def own_high(step):
        return remote(x_ref.at[0, :, hi], xg.at[y, z, :, hi], bz_ss.at[0], bz_rs.at[step % Z - 1], "z", step)

    def low(j, off, step):
        yb, zb = shifted("y", -j), shifted("z", -off)
        src = x_ref.at[0, :, lo] if j == 0 and off == 0 else xg.at[yb, zb, :, lo]
        to = (off + step) % Z
        at = 7 + (to == 6) * 4 + j if to in (2, 6) else to - 1
        return remote(src, xg.at[yb, zb, :, lo], az_ss.at[0], az_rs.at[at], "z", step)

    def spread_z(j):
        for step in (2, -2, 1, -1):
            low(j, 0, step).start()

    def relay_low(j):
        for sign in (1, -1):
            low(j, 0, 2 * sign).wait_recv()
            long = sign == (1 if j % 2 == 0 else -1)
            for step in (2, 1) if long else (1,):
                low(j, 2 * sign, step * sign).start()

    def across(j, i):
        zb = shifted("z", -j)
        src = x_ref.at[0, :, hi] if j == 0 else xg.at[y, zb, :, hi]
        return remote(src, xg.at[y, zb, :, hi], by_ss.at[0], by_rs.at[i - 1], "y", i)

    def spread(j):
        for i in (1, 3, 2):
            across(j, i).start()

    for i in (1, 3, 2):
        gy(i).start()
    for step in (2, -2, 1, -1):
        own_high(step).start()
    spread(0)
    spread_z(0)

    enc_push = remote(enc_ref.at[0], wenc.at[c], w_ss.at[0], w_rs.at[0], "c", 1)
    eb_push = remote(eb_ref, ebv.at[c], w_ss.at[1], w_rs.at[1], "c", 1)

    def push_weights():
        enc_push.start()
        eb_push.start()
        each_k(lambda k: dec_push(k).start())

    @pl.when(c == 0)
    def _():
        pl.semaphore_wait(partner_sem, 1)

    push_weights()

    def take_y(i):
        gy(i).wait_recv()
        spread_z(i)

    turn = 1 - 2 * lax.rem(y, 2)

    def take_z(off):
        own_high(off).wait_recv()
        spread(off)

    def relay_z(off):
        own_high(off).wait_recv()
        sign = 1 if off == 2 else -1
        high(2 * sign, sign).start()

        @pl.when(turn == sign)
        def _():
            high(2 * sign, 2 * sign).start()

        spread(off)

    take_y(1), take_y(3), take_z(1), take_z(7), relay_z(2), relay_z(6), relay_low(0), take_y(2), relay_low(1), relay_low(3)
    take_z(3), take_z(5), take_z(4), relay_low(2)

    def all_across(i):
        block = xg.at[y, :, :, hi]
        return remote(block, block, by_ss.at[0], by_rs.at[i - 1], "y", i)

    def all_along(i):
        block = xg.at[:, z, :, lo]
        return remote(block, block, az_ss.at[0], az_rs.at[i - 1], "z", i)

    for i in (1, 3, 2):
        all_across(i).wait_recv()
    for i in (1, 7, 3, 5, 4):
        all_along(i).wait_recv()
    for cp in locals_:
        cp.wait()
    enc_push.wait_recv()
    eb_push.wait_recv()

    rows = xg[...].astype(jnp.float32).reshape(Z * Y * ROWS, D).astype(jnp.bfloat16)
    for side in range(C):
        for n in range(FEATS // TILE):
            at = pl.ds(n * TILE, TILE)
            pre = jnp.dot(rows, wenc[side, :, at], preferred_element_type=jnp.float32) + ebv[side, :, at]
            act[:, pl.ds(side * FEATS + n * TILE, TILE)] = jnp.maximum(pre, 0.0).astype(jnp.bfloat16)

    def product(k, col):
        at = pl.ds(col, TILE)
        weight = wdec[k, :, :, at].reshape(C * FEATS, TILE)
        out = jnp.dot(act[...], weight, preferred_element_type=jnp.float32)
        return out.reshape(Y, Z, ROWS, TILE)

    ready = set()

    def dec_ready(k):
        if k not in ready:
            ready.add(k)
            dec_local(k).wait()
            dec_push(k).wait_recv()

    def move(i, n):
        at = pl.ds(n * TILE, TILE)
        return remote(mvs.at[i, :, :, :, at], mvr.at[i, :, :, :, at], mv_ss.at[i], mv_rs.at[i, n], "x", 1 - 2 * i)

    def moved(k):
        i = k // 2
        dec_ready(k)
        for n in (0, 1, 2, 3):
            mvs[i, :, :, :, pl.ds(n * TILE, TILE)] = product(k, B_COLS + n * TILE).astype(jnp.bfloat16)
            move(i, n).start()

    def own1(g, k, d):
        cols = pl.ds(g.start, g.width)
        return part[k, d, :, :, cols] if g.first == "y" else part[k, :, d, :, cols]

    def own2(g, j, d):
        return g.t[j, d]

    def copy1(g, j, slot, step):
        return remote(g.s1.at[j, slot], g.r1.at[j, slot], g.ss1.at[j], g.rs1.at[j, slot], g.first, step)

    def copy2(g, j, slot, step):
        return remote(g.s2.at[j, slot], g.r2.at[j, slot], g.ss2.at[j], g.rs2.at[j, 0 if g.direct else slot], g.second, step)

    def stage_of(g, stage, j, k):
        if stage == 1:
            return g.first, g.n1, (lambda d: own1(g, k, d)), g.s1, g.r1, (lambda slot, step: copy1(g, j, slot, step))
        return g.second, g.n2, (lambda d: own2(g, j, d)), g.s2, g.r2, (lambda slot, step: copy2(g, j, slot, step))

    done = {}

    def chain_step(i, stage, k, long, s):
        g = gs[i]
        j = k if g.ks == X else k // 2
        axis, size, own, sref, rref, copy = stage_of(g, stage, j, k)
        half = size // 2
        hops, base = (half, 0) if long else (half - 1, half)
        step = (1 if j % 2 == 0 else -1) * (1 if long else -1)
        if s > 0:
            copy(base + s - 1, step).wait_recv()
        if s < hops:
            msg = own(shifted(axis, step * (hops - s)))
            if s > 0:
                msg = msg + rref[j, base + s - 1].astype(jnp.float32)
            sref[j, base + s] = msg.astype(jnp.bfloat16)
            copy(base + s, step).start()
            return
        done[i, stage, k] = done.get((i, stage, k), 0) + 1
        if done[i, stage, k] == 2:
            total = own(lax.axis_index(axis)) + rref[j, half - 1].astype(jnp.float32) + rref[j, size - 2].astype(jnp.float32)
            if stage == 2:
                fin[k, :, pl.ds(g.start, g.width)] = total
                return
            g.t[j] = total
            if g.direct:
                direct_send(g, j)
            else:
                begin(i, 2, k)

    def begin(i, stage, k):
        chain_step(i, stage, k, True, 0)
        chain_step(i, stage, k, False, 0)

    def direct_send(g, j):
        for o in sorted(range(1, g.n2), key=lambda o: -min(o, g.n2 - o)):
            g.s2[j, o - 1] = own2(g, j, shifted(g.second, o)).astype(jnp.bfloat16)
            copy2(g, j, o - 1, o).start()

    def direct_sum(i, k):
        g = gs[i]
        j = k if g.ks == X else k // 2
        remote(g.s2.at[j], g.r2.at[j], g.ss2.at[j], g.rs2.at[j, 0], g.second, 1).wait_recv()
        total = own2(g, j, lax.axis_index(g.second))
        for o in range(1, g.n2):
            total = total + g.r2[j, o - 1].astype(jnp.float32)
        fin[k, :, pl.ds(g.start, g.width)] = total

    def low_columns(k):
        dec_ready(k)
        for n in range(B_COLS // TILE):
            part[k, :, :, :, pl.ds(n * TILE, TILE)] = product(k, n * TILE)
        begin(0, 1, k)
        begin(1, 1, k)

    def high_columns(k):
        dec_ready(k)
        for n in range(A_COLS // TILE):
            at = B_COLS + n * TILE
            part[k, :, :, :, pl.ds(at, TILE)] = product(k, at)
        if k:
            begin(2, 1, k)

    def join(i, n):
        move(i, n).wait_recv()
        at = pl.ds(B_COLS + n * TILE, TILE)
        part[0, :, :, :, at] = part[0, :, :, :, at] + mvr[i, :, :, :, pl.ds(n * TILE, TILE)].astype(jnp.float32)

    def own_target(i):
        tiles = range((gs[i].start - B_COLS) // TILE, (gs[i].start - B_COLS + gs[i].width) // TILE)
        pl.when(l > 0)(lambda: [join(0, n) for n in tiles] and None)
        pl.when(l == X - 1)(lambda: [join(1, n) for n in tiles] and None)
        begin(i, 1, 0)

    def late(k, is_a):
        at = pl.ds(B_COLS, A_COLS) if is_a else pl.ds(0, B_COLS)
        slot = 3 if is_a else k - 1
        return remote(fsend.at[k - 1, :, at], frecv.at[k - 1, :, at], f_ss.at[slot], f_rs.at[slot], "x", k)

    def send_late(k, is_a):
        at = pl.ds(B_COLS, A_COLS) if is_a else pl.ds(0, B_COLS)
        fsend[k - 1, :, at] = fin[k, :, at].astype(jnp.bfloat16)
        late(k, is_a).start()

    left = {(k, is_a): 1 if is_a else 2 for k in range(X) for is_a in (False, True)}

    def run(kind, *rest):
        k = rest[2] if kind == 4 else rest[1] if kind == 5 else 0 if kind == 3 else rest[0]

        def act_():
            if kind == 0:
                low_columns(k)
            elif kind == 1:
                moved(k)
            elif kind == 2:
                high_columns(k)
            elif kind == 3:
                own_target(rest[0])
            else:
                if kind == 4:
                    chain_step(*rest)
                else:
                    direct_sum(*rest)
                i = rest[0]
                last = kind == 5 or (rest[1] == 2 and done.get((i, 2, k), 0) == 2)
                if last:
                    left[k, i >= 2] -= 1
                    if k and not left[k, i >= 2]:
                        send_late(k, i >= 2)

        if k == 0:
            act_()
        else:
            pl.when(l + k < X)(act_)

    for step in ORDER:
        run(*step)

    def take_late(k, is_a):
        late(k, is_a).wait_recv()
        at = pl.ds(B_COLS, A_COLS) if is_a else pl.ds(0, B_COLS)
        fin[0, :, at] = fin[0, :, at] + frecv[k - 1, :, at].astype(jnp.float32)

    for k in (1, 2, 3):
        pl.when(l >= k)(lambda k=k: take_late(k, False))
    pl.when(l >= 2)(lambda: take_late(2, True))
    o_ref[0] = (fin[0] + db_ref[...]).astype(jnp.bfloat16)

    def left_all(src, send, recv):
        remote(src, src, send, recv, "y", 1).wait_send()

    left_all(xg.at[0, pl.ds(0, 3), :, lo], ay_ss.at[0], ay_rs.at[0])
    left_all(xg.at[:, pl.ds(0, 7), :, lo], az_ss.at[0], az_rs.at[0])
    left_all(xg.at[0, pl.ds(0, 7), :, hi], bz_ss.at[0], bz_rs.at[0])
    left_all(xg.at[pl.ds(0, 3), :, :, hi], by_ss.at[0], by_rs.at[0])
    enc_push.wait_send()
    eb_push.wait_send()
    each_k(lambda k: dec_push(k).wait_send())
    each_k(lambda k: left_all(mvs.at[k // 2], mv_ss.at[k // 2], mv_rs.at[k // 2, 0]), (1, 3))
    each_k(lambda k: late(k, False).wait_send(), (1, 2, 3))
    pl.when(l < 2)(lambda: late(2, True).wait_send())

    def drain(g, j):
        left_all(g.s1.at[j], g.ss1.at[j], g.rs1.at[j, 0])
        left_all(g.s2.at[j], g.ss2.at[j], g.rs2.at[j, 0])

    each_k(lambda k: [drain(g, k if g.ks == X else k // 2) for g in gs if g.ks == X or k % 2 == 0] and None)


def per_device(resid_in, enc_weight, enc_bias, dec_weight, dec_bias):
    dma = pltpu.SemaphoreType.DMA
    scratch = [
        pltpu.VMEM((C, D, FEATS), jnp.bfloat16),
        pltpu.VMEM((X, C, FEATS, D), jnp.bfloat16),
        pltpu.VMEM((C, 1, FEATS), jnp.float32),
        pltpu.VMEM((Y, Z, ROWS, D), jnp.bfloat16),
        pltpu.VMEM((Z * Y * ROWS, C * FEATS), jnp.bfloat16),
        pltpu.VMEM((X, Y, Z, ROWS, D), jnp.float32),
        pltpu.VMEM((2, Y, Z, ROWS, A_COLS), jnp.bfloat16),
        pltpu.VMEM((2, Y, Z, ROWS, A_COLS), jnp.bfloat16),
        pltpu.VMEM((X, ROWS, D), jnp.float32),
        pltpu.VMEM((X - 1, ROWS, D), jnp.bfloat16),
        pltpu.VMEM((X - 1, ROWS, D), jnp.bfloat16),
        dma((7,)),
        dma((6,)), dma((6,)),
        dma((1,)), dma((3,)),
        dma((1,)), dma((15,)),
        dma((1,)), dma((7,)),
        dma((1,)), dma((3,)),
        dma((2,)), dma((2, A_COLS // TILE)),
        dma((4,)), dma((4,)),
        pltpu.SemaphoreType.REGULAR,
    ]
    for g in groups():
        scratch += g.scratch()
    anywhere = pl.BlockSpec(memory_space=pl.ANY)
    return pl.pallas_call(
        kernel,
        out_shape=jax.ShapeDtypeStruct((1, ROWS, D), jnp.bfloat16),
        in_specs=[anywhere, anywhere, anywhere, anywhere, pl.BlockSpec(memory_space=pltpu.VMEM)],
        out_specs=pl.BlockSpec(memory_space=pltpu.VMEM),
        scratch_shapes=scratch,
        compiler_params=pltpu.CompilerParams(collective_id=0, has_side_effects=True, vmem_limit_bytes=67043328),
        name="transcoder",
    )(resid_in, enc_weight, enc_bias, dec_weight, dec_bias)


def solution(mesh):
    finer = Mesh(mesh.devices.reshape(Z, Y, C, X), ("z", "y", "c", "x"))
    return jax.shard_map(
        per_device,
        mesh=finer,
        in_specs=(
            P("x", FEAT, None),
            P("x", None, FEAT),
            P("x", FEAT),
            P("x", None, FEAT, None),
            P("x", None),
        ),
        out_specs=P("x", FEAT, None),
        check_vma=False,
    )
```

```python
import jax
import jax.numpy as jnp
from jax import lax
from jax.experimental import pallas as pl
from jax.experimental.pallas import tpu as pltpu
from jax.sharding import Mesh
from jax.sharding import PartitionSpec as P

FEAT = ("z", "y", "c")
MESH = pl.DeviceIdType.MESH
Z, Y, C, X = 8, 4, 2, 4
SIZE = {"z": Z, "y": Y, "c": C, "x": X}
ROWS = 8
D = 2304
FEATS = 512
TILE = 256
GATHER_SPLIT = 768
B_COLS = 1280
A_COLS = D - B_COLS

ORDER = (
    (0,1), (1,1), (1,3), (4,1,1,1,1,1), (4,1,1,1,0,1), (4,0,1,1,1,1), (4,0,1,1,0,1), (0,3), (0,2), (2,2), (4,1,1,1,1,2),
    (4,1,1,1,0,2), (0,0), (4,0,1,1,1,2), (4,1,1,3,1,1), (4,1,1,3,0,1), (4,0,1,3,0,1), (4,0,1,3,1,1), (2,0), (4,1,1,2,1,1),
    (4,1,1,2,0,1), (4,0,1,2,1,1), (4,0,1,2,0,1), (4,1,1,1,1,3), (4,1,1,1,0,3), (4,1,1,0,1,1), (4,1,1,0,0,1), (4,2,1,2,0,1),
    (4,2,1,2,1,1), (4,1,1,3,0,2), (4,0,1,0,1,1), (4,0,1,0,0,1), (4,1,1,3,1,2), (4,1,1,2,1,2), (3,2), (4,0,1,2,1,2), (4,0,1,3,1,2),
    (5,0,1), (4,1,1,2,0,2), (4,1,1,0,1,2), (4,1,1,1,1,4), (4,1,1,3,0,3), (4,1,1,0,0,2), (4,0,1,0,1,2), (4,2,1,2,1,2), (4,1,1,2,1,3),
    (4,1,1,3,1,3), (4,2,1,0,1,1), (4,2,1,0,0,1), (5,0,2), (4,1,1,0,1,3), (4,1,1,2,0,3), (5,1,1), (5,0,3), (4,1,1,0,0,3), (5,0,0),
    (4,2,1,0,1,2), (4,1,1,2,1,4), (4,1,1,0,1,4), (5,2,2), (4,1,1,3,1,4), (5,1,2), (5,1,0), (5,1,3), (5,2,0),
)

class Group:
    def __init__(self, first, start, width, ks, direct):
        self.first, self.second = first, "y" if first == "z" else "z"
        self.start, self.width, self.ks = start, width, ks
        self.n1, self.n2 = SIZE[self.first], SIZE[self.second]
        self.direct = direct

    def scratch(self):
        k, n1, n2, w = self.ks, self.n1, self.n2, self.width
        return [
            pltpu.VMEM((k, n1 - 1, n2, ROWS, w), jnp.bfloat16),
            pltpu.VMEM((k, n1 - 1, n2, ROWS, w), jnp.bfloat16),
            pltpu.VMEM((k, n2, ROWS, w), jnp.float32),
            pltpu.VMEM((k, n2 - 1, ROWS, w), jnp.bfloat16),
            pltpu.VMEM((k, n2 - 1, ROWS, w), jnp.bfloat16),
            pltpu.SemaphoreType.DMA((k,)),
            pltpu.SemaphoreType.DMA((k, n1 - 1)),
            pltpu.SemaphoreType.DMA((k,)),
            pltpu.SemaphoreType.DMA((k, 1 if self.direct else n2 - 1)),
        ]

    def bind(self, refs):
        (self.s1, self.r1, self.t, self.s2, self.r2, self.ss1, self.rs1, self.ss2, self.rs2) = refs


def groups():
    return [
        Group("y", 0, 512, 4, True),
        Group("z", 512, 768, 4, True),
        Group("y", 1280, 1024, 2, True),
    ]


def shifted(axis, step):
    return lax.rem(lax.axis_index(axis) + step + 2 * SIZE[axis], SIZE[axis])


def remote(src, dst, send, recv, axis, step):
    return pltpu.make_async_remote_copy(
        src_ref=src, dst_ref=dst, send_sem=send, recv_sem=recv,
        device_id={axis: shifted(axis, step)}, device_id_type=MESH,
    )


def kernel(x_ref, enc_ref, eb_ref, dec_ref, db_ref, o_ref, wenc, wdec, ebv, xg, act, part, mvs, mvr, fin, fsend, frecv,
           local_sem, w_ss, w_rs, ay_ss, ay_rs, az_ss, az_rs, bz_ss, bz_rs, by_ss, by_rs, mv_ss, mv_rs, f_ss, f_rs, partner_sem, *rest):
    gs = groups()
    for i, g in enumerate(gs):
        g.bind(rest[9 * i : 9 * i + 9])
    z, y, c, l = (lax.axis_index(a) for a in ("z", "y", "c", "x"))

    locals_ = [
        pltpu.make_async_copy(enc_ref.at[0], wenc.at[c], local_sem.at[0]),
        pltpu.make_async_copy(eb_ref, ebv.at[c], local_sem.at[1]),
        pltpu.make_async_copy(x_ref.at[0], xg.at[y, z], local_sem.at[2]),
    ]
    for cp in locals_:
        cp.start()

    def dec_local(k):
        return pltpu.make_async_copy(dec_ref.at[0, l + k], wdec.at[k, c], local_sem.at[3 + k])

    def dec_push(k):
        return remote(dec_ref.at[0, l + k], wdec.at[k, c], w_ss.at[2 + k], w_rs.at[2 + k], "c", 1)

    def each_k(fn, order=(1, 3, 2, 0)):
        for k in order:
            if k == 0:
                fn(0)
            else:
                pl.when(l + k < X)(lambda k=k: fn(k))

    each_k(lambda k: dec_local(k).start())

    bar = pltpu.get_barrier_semaphore()
    peers = [("y", i) for i in (1, 2, 3)] + [("z", i) for i in (1, 2, 6, 7)] + [("x", i) for i in (1, 2, 3)]

    @pl.when(c == 0)
    def _():
        pl.semaphore_signal(bar, inc=1, device_id={"c": 1}, device_id_type=MESH)

    for a, i in peers:
        pl.semaphore_signal(bar, inc=1, device_id={a: shifted(a, i)}, device_id_type=MESH)
    pl.semaphore_wait(bar, len(peers) + c)

    @pl.when(c == 1)
    def _():
        pl.semaphore_signal(partner_sem, inc=1, device_id={"c": 0}, device_id_type=MESH)

    lo, hi = pl.ds(0, GATHER_SPLIT), pl.ds(GATHER_SPLIT, D - GATHER_SPLIT)

    def gy(i):
        return remote(x_ref.at[0, :, lo], xg.at[y, z, :, lo], ay_ss.at[0], ay_rs.at[i - 1], "y", i)

    def high(off, step):
        zb = shifted("z", -off)
        at = lax.rem(off + step + 2 * Z, Z) - 1
        return remote(xg.at[y, zb, :, hi], xg.at[y, zb, :, hi], bz_ss.at[0], bz_rs.at[at], "z", step)

    def own_high(step):
        return remote(x_ref.at[0, :, hi], xg.at[y, z, :, hi], bz_ss.at[0], bz_rs.at[step % Z - 1], "z", step)

    def low(j, off, step):
        yb, zb = shifted("y", -j), shifted("z", -off)
        src = x_ref.at[0, :, lo] if j == 0 and off == 0 else xg.at[yb, zb, :, lo]
        to = (off + step) % Z
        at = 7 + (to == 6) * 4 + j if to in (2, 6) else to - 1
        return remote(src, xg.at[yb, zb, :, lo], az_ss.at[0], az_rs.at[at], "z", step)

    def spread_z(j):
        for step in (2, -2, 1, -1):
            low(j, 0, step).start()

    def relay_low(j):
        for sign in (1, -1):
            low(j, 0, 2 * sign).wait_recv()
            long = sign == (1 if j % 2 == 0 else -1)
            for step in (2, 1) if long else (1,):
                low(j, 2 * sign, step * sign).start()

    def across(j, i):
        zb = shifted("z", -j)
        src = x_ref.at[0, :, hi] if j == 0 else xg.at[y, zb, :, hi]
        return remote(src, xg.at[y, zb, :, hi], by_ss.at[0], by_rs.at[i - 1], "y", i)

    def spread(j):
        for i in (1, 3, 2):
            across(j, i).start()

    for i in (1, 3, 2):
        gy(i).start()
    for step in (2, -2, 1, -1):
        own_high(step).start()
    spread(0)
    spread_z(0)

    enc_push = remote(enc_ref.at[0], wenc.at[c], w_ss.at[0], w_rs.at[0], "c", 1)
    eb_push = remote(eb_ref, ebv.at[c], w_ss.at[1], w_rs.at[1], "c", 1)

    def push_weights():
        enc_push.start()
        eb_push.start()
        each_k(lambda k: dec_push(k).start())

    @pl.when(c == 0)
    def _():
        pl.semaphore_wait(partner_sem, 1)

    push_weights()

    def take_y(i):
        gy(i).wait_recv()
        spread_z(i)

    turn = 1 - 2 * lax.rem(y, 2)

    def take_z(off):
        own_high(off).wait_recv()
        spread(off)

    def relay_z(off):
        own_high(off).wait_recv()
        sign = 1 if off == 2 else -1
        high(2 * sign, sign).start()

        @pl.when(turn == sign)
        def _():
            high(2 * sign, 2 * sign).start()

        spread(off)

    take_y(1), take_y(3), take_z(1), take_z(7), relay_z(2), relay_z(6), relay_low(0), take_y(2), relay_low(1), relay_low(3)
    take_z(3), take_z(5), take_z(4), relay_low(2)

    def all_across(i):
        block = xg.at[y, :, :, hi]
        return remote(block, block, by_ss.at[0], by_rs.at[i - 1], "y", i)

    def all_along(i):
        block = xg.at[:, z, :, lo]
        return remote(block, block, az_ss.at[0], az_rs.at[i - 1], "z", i)

    for i in (1, 3, 2):
        all_across(i).wait_recv()
    for i in (1, 7, 3, 5, 4):
        all_along(i).wait_recv()
    for cp in locals_:
        cp.wait()
    enc_push.wait_recv()
    eb_push.wait_recv()

    rows = xg[...].astype(jnp.float32).reshape(Z * Y * ROWS, D).astype(jnp.bfloat16)
    for side in range(C):
        for n in range(FEATS // TILE):
            at = pl.ds(n * TILE, TILE)
            pre = jnp.dot(rows, wenc[side, :, at], preferred_element_type=jnp.float32) + ebv[side, :, at]
            act[:, pl.ds(side * FEATS + n * TILE, TILE)] = jnp.maximum(pre, 0.0).astype(jnp.bfloat16)

    def product(k, col):
        at = pl.ds(col, TILE)
        weight = wdec[k, :, :, at].reshape(C * FEATS, TILE)
        out = jnp.dot(act[...], weight, preferred_element_type=jnp.float32)
        return out.reshape(Y, Z, ROWS, TILE)

    ready = set()

    def dec_ready(k):
        if k not in ready:
            ready.add(k)
            dec_local(k).wait()
            dec_push(k).wait_recv()

    def move(i, n):
        at = pl.ds(n * TILE, TILE)
        return remote(mvs.at[i, :, :, :, at], mvr.at[i, :, :, :, at], mv_ss.at[i], mv_rs.at[i, n], "x", 1 - 2 * i)

    def moved(k):
        i = k // 2
        dec_ready(k)
        for n in (0, 1, 2, 3):
            mvs[i, :, :, :, pl.ds(n * TILE, TILE)] = product(k, B_COLS + n * TILE).astype(jnp.bfloat16)
            move(i, n).start()

    def own1(g, k, d):
        cols = pl.ds(g.start, g.width)
        return part[k, d, :, :, cols] if g.first == "y" else part[k, :, d, :, cols]

    def own2(g, j, d):
        return g.t[j, d]

    def copy1(g, j, slot, step):
        return remote(g.s1.at[j, slot], g.r1.at[j, slot], g.ss1.at[j], g.rs1.at[j, slot], g.first, step)

    def copy2(g, j, slot, step):
        return remote(g.s2.at[j, slot], g.r2.at[j, slot], g.ss2.at[j], g.rs2.at[j, 0 if g.direct else slot], g.second, step)

    def stage_of(g, stage, j, k):
        if stage == 1:
            return g.first, g.n1, (lambda d: own1(g, k, d)), g.s1, g.r1, (lambda slot, step: copy1(g, j, slot, step))
        return g.second, g.n2, (lambda d: own2(g, j, d)), g.s2, g.r2, (lambda slot, step: copy2(g, j, slot, step))

    done = {}

    def chain_step(i, stage, k, long, s):
        g = gs[i]
        j = k if g.ks == X else k // 2
        axis, size, own, sref, rref, copy = stage_of(g, stage, j, k)
        half = size // 2
        hops, base = (half, 0) if long else (half - 1, half)
        step = (1 if j % 2 == 0 else -1) * (1 if long else -1)
        if s > 0:
            copy(base + s - 1, step).wait_recv()
        if s < hops:
            msg = own(shifted(axis, step * (hops - s)))
            if s > 0:
                msg = msg + rref[j, base + s - 1].astype(jnp.float32)
            sref[j, base + s] = msg.astype(jnp.bfloat16)
            copy(base + s, step).start()
            return
        done[i, stage, k] = done.get((i, stage, k), 0) + 1
        if done[i, stage, k] == 2:
            total = own(lax.axis_index(axis)) + rref[j, half - 1].astype(jnp.float32) + rref[j, size - 2].astype(jnp.float32)
            if stage == 2:
                fin[k, :, pl.ds(g.start, g.width)] = total
                return
            g.t[j] = total
            if g.direct:
                direct_send(g, j)
            else:
                begin(i, 2, k)

    def begin(i, stage, k):
        chain_step(i, stage, k, True, 0)
        chain_step(i, stage, k, False, 0)

    def direct_send(g, j):
        for o in sorted(range(1, g.n2), key=lambda o: -min(o, g.n2 - o)):
            g.s2[j, o - 1] = own2(g, j, shifted(g.second, o)).astype(jnp.bfloat16)
            copy2(g, j, o - 1, o).start()

    def direct_sum(i, k):
        g = gs[i]
        j = k if g.ks == X else k // 2
        remote(g.s2.at[j], g.r2.at[j], g.ss2.at[j], g.rs2.at[j, 0], g.second, 1).wait_recv()
        total = own2(g, j, lax.axis_index(g.second))
        for o in range(1, g.n2):
            total = total + g.r2[j, o - 1].astype(jnp.float32)
        fin[k, :, pl.ds(g.start, g.width)] = total

    def low_columns(k):
        dec_ready(k)
        for n in range(B_COLS // TILE):
            part[k, :, :, :, pl.ds(n * TILE, TILE)] = product(k, n * TILE)
        begin(0, 1, k)
        begin(1, 1, k)

    def high_columns(k):
        dec_ready(k)
        for n in range(A_COLS // TILE):
            at = B_COLS + n * TILE
            part[k, :, :, :, pl.ds(at, TILE)] = product(k, at)
        if k:
            begin(2, 1, k)

    def join(i, n):
        move(i, n).wait_recv()
        at = pl.ds(B_COLS + n * TILE, TILE)
        part[0, :, :, :, at] = part[0, :, :, :, at] + mvr[i, :, :, :, pl.ds(n * TILE, TILE)].astype(jnp.float32)

    def own_target(i):
        tiles = range((gs[i].start - B_COLS) // TILE, (gs[i].start - B_COLS + gs[i].width) // TILE)
        pl.when(l > 0)(lambda: [join(0, n) for n in tiles] and None)
        pl.when(l == X - 1)(lambda: [join(1, n) for n in tiles] and None)
        begin(i, 1, 0)

    def late(k, is_a):
        at = pl.ds(B_COLS, A_COLS) if is_a else pl.ds(0, B_COLS)
        slot = 3 if is_a else k - 1
        return remote(fsend.at[k - 1, :, at], frecv.at[k - 1, :, at], f_ss.at[slot], f_rs.at[slot], "x", k)

    def send_late(k, is_a):
        at = pl.ds(B_COLS, A_COLS) if is_a else pl.ds(0, B_COLS)
        fsend[k - 1, :, at] = fin[k, :, at].astype(jnp.bfloat16)
        late(k, is_a).start()

    left = {(k, is_a): 1 if is_a else 2 for k in range(X) for is_a in (False, True)}

    def run(kind, *rest):
        k = rest[2] if kind == 4 else rest[1] if kind == 5 else 0 if kind == 3 else rest[0]

        def act_():
            if kind == 0:
                low_columns(k)
            elif kind == 1:
                moved(k)
            elif kind == 2:
                high_columns(k)
            elif kind == 3:
                own_target(rest[0])
            else:
                if kind == 4:
                    chain_step(*rest)
                else:
                    direct_sum(*rest)
                i = rest[0]
                last = kind == 5 or (rest[1] == 2 and done.get((i, 2, k), 0) == 2)
                if last:
                    left[k, i >= 2] -= 1
                    if k and not left[k, i >= 2]:
                        send_late(k, i >= 2)

        if k == 0:
            act_()
        else:
            pl.when(l + k < X)(act_)

    for step in ORDER:
        run(*step)

    def take_late(k, is_a):
        late(k, is_a).wait_recv()
        at = pl.ds(B_COLS, A_COLS) if is_a else pl.ds(0, B_COLS)
        fin[0, :, at] = fin[0, :, at] + frecv[k - 1, :, at].astype(jnp.float32)

    for k in (1, 2, 3):
        pl.when(l >= k)(lambda k=k: take_late(k, False))
    pl.when(l >= 2)(lambda: take_late(2, True))
    o_ref[0] = (fin[0] + db_ref[...]).astype(jnp.bfloat16)

    def left_all(src, send, recv):
        remote(src, src, send, recv, "y", 1).wait_send()

    left_all(xg.at[0, pl.ds(0, 3), :, lo], ay_ss.at[0], ay_rs.at[0])
    left_all(xg.at[:, pl.ds(0, 7), :, lo], az_ss.at[0], az_rs.at[0])
    left_all(xg.at[0, pl.ds(0, 7), :, hi], bz_ss.at[0], bz_rs.at[0])
    left_all(xg.at[pl.ds(0, 3), :, :, hi], by_ss.at[0], by_rs.at[0])
    enc_push.wait_send()
    eb_push.wait_send()
    each_k(lambda k: dec_push(k).wait_send())
    each_k(lambda k: left_all(mvs.at[k // 2], mv_ss.at[k // 2], mv_rs.at[k // 2, 0]), (1, 3))
    each_k(lambda k: late(k, False).wait_send(), (1, 2, 3))
    pl.when(l < 2)(lambda: late(2, True).wait_send())

    def drain(g, j):
        left_all(g.s1.at[j], g.ss1.at[j], g.rs1.at[j, 0])
        left_all(g.s2.at[j], g.ss2.at[j], g.rs2.at[j, 0])

    each_k(lambda k: [drain(g, k if g.ks == X else k // 2) for g in gs if g.ks == X or k % 2 == 0] and None)


def per_device(resid_in, enc_weight, enc_bias, dec_weight, dec_bias):
    dma = pltpu.SemaphoreType.DMA
    scratch = [
        pltpu.VMEM((C, D, FEATS), jnp.bfloat16),
        pltpu.VMEM((X, C, FEATS, D), jnp.bfloat16),
        pltpu.VMEM((C, 1, FEATS), jnp.float32),
        pltpu.VMEM((Y, Z, ROWS, D), jnp.bfloat16),
        pltpu.VMEM((Z * Y * ROWS, C * FEATS), jnp.bfloat16),
        pltpu.VMEM((X, Y, Z, ROWS, D), jnp.float32),
        pltpu.VMEM((2, Y, Z, ROWS, A_COLS), jnp.bfloat16),
        pltpu.VMEM((2, Y, Z, ROWS, A_COLS), jnp.bfloat16),
        pltpu.VMEM((X, ROWS, D), jnp.float32),
        pltpu.VMEM((X - 1, ROWS, D), jnp.bfloat16),
        pltpu.VMEM((X - 1, ROWS, D), jnp.bfloat16),
        dma((7,)),
        dma((6,)), dma((6,)),
        dma((1,)), dma((3,)),
        dma((1,)), dma((15,)),
        dma((1,)), dma((7,)),
        dma((1,)), dma((3,)),
        dma((2,)), dma((2, A_COLS // TILE)),
        dma((4,)), dma((4,)),
        pltpu.SemaphoreType.REGULAR,
    ]
    for g in groups():
        scratch += g.scratch()
    anywhere = pl.BlockSpec(memory_space=pl.ANY)
    return pl.pallas_call(
        kernel,
        out_shape=jax.ShapeDtypeStruct((1, ROWS, D), jnp.bfloat16),
        in_specs=[anywhere, anywhere, anywhere, anywhere, pl.BlockSpec(memory_space=pltpu.VMEM)],
        out_specs=pl.BlockSpec(memory_space=pltpu.VMEM),
        scratch_shapes=scratch,
        compiler_params=pltpu.CompilerParams(collective_id=0, has_side_effects=True, vmem_limit_bytes=67043328),
        name="transcoder",
    )(resid_in, enc_weight, enc_bias, dec_weight, dec_bias)


def solution(mesh):
    finer = Mesh(mesh.devices.reshape(Z, Y, C, X), ("z", "y", "c", "x"))
    return jax.shard_map(
        per_device,
        mesh=finer,
        in_specs=(
            P("x", FEAT, None),
            P("x", None, FEAT),
            P("x", FEAT),
            P("x", None, FEAT, None),
            P("x", None),
        ),
        out_specs=P("x", FEAT, None),
        check_vma=False,
    )
```
